32 devices in a mesh: sx: 4 (over x, core), sy: 8 (over z, y).
Axes of the slice: x: 2, y: 2, z: 4, core: 2. Of those that a mesh axis runs over, the one named last changes fastest.
Arguments:
- right_side: float32 [8, 8, 8, 8192], P(None, None, None, ('sx', 'sy')), may hold values from -8 to 8
- stretch: float32 [3, 8192], P(None, ('sx', 'sy')), may hold values from 0.3 to 3
- mass_term: float32 [8192], P(('sx', 'sy')), may hold values from 0.5 to 2
- slot_position: int32 [8192], P(('sx', 'sy')), may hold values from 0 to 255, as said below
- coarse_group: int32 [8192], P(('sx', 'sy')), may hold values from 0 to 511, as said below
Outputs:
- smoothed: float32 [8, 8, 8, 8192], P(None, None, None, ('sx', 'sy'))
- fine_residual: float32 [8, 8, 8, 8192], P(None, None, None, ('sx', 'sy'))
- coarse_rhs: float32 [8, 512], P(None, ('sx', 'sy'))
The draws below stay inside these ranges and needn't reach their ends.
Inputs may be any that keep to these rules, and one draw needn't show every extreme that they name: `slot_position`: each device's block of 256 entries is a permutation of 0 to 255. `coarse_group`: group k is owned by the device of block index k // 16 (block index i * 8 + j); an element of device (i, j) belongs to a group owned by some device (i, j') of the same first index.
All inputs are finite; a program needn't handle non-finite values.
Results may differ from the reference program's by a relative error of at most 0.00013.
Values sent between devices are 32-bit elements; how exact they have to be, the bound alone decides.
A program may use at most 128 MiB of HBM per device.

```python
import math
import jax
import jax.numpy as jnp
from jax import lax

NODES = 8
SWEEPS = 2
EX = 1
EY = 2
EZ = 128
GRP_DEV = 16
E_DEV = 256
ELEMENTS = 8192
GROUPS = 512
N_SX = 4
N_SY = 8
DEVICES = 32


def draw_slot_position(key, part):
    base = jax.random.fold_in(key, 11)
    keys = jax.vmap(lambda number: jax.random.fold_in(base, number))(jnp.arange(DEVICES))
    orders = jax.vmap(lambda single: jax.random.permutation(single, EX * EY * EZ))(keys)
    return orders.reshape(-1).astype(jnp.int32)


def draw_coarse_group(key, part):
    element = jnp.arange(ELEMENTS, dtype=jnp.int32)
    device = element // E_DEV
    local = element % E_DEV
    row_index = device // N_SY
    col_index = device % N_SY
    offset = jax.random.randint(jax.random.fold_in(key, 21), (ELEMENTS,), 0, N_SY)
    offset = jnp.where(local == 0, N_SY // 2, offset)
    offset = jnp.where(local == 1, 1, offset)
    owner_col = (col_index + offset) % N_SY
    member = jax.random.randint(jax.random.fold_in(key, 22), (ELEMENTS,), 0, GRP_DEV)
    return ((row_index * N_SY + owner_col) * GRP_DEV + member).astype(jnp.int32)


def levels(rng, shape, split, low, largest):
    def one(dim, blocks):
        steps = jax.random.uniform(jax.random.fold_in(jax.random.fold_in(rng, 6), dim), (blocks,), jnp.float32, low / len(split), largest / len(split))
        return jnp.repeat(jnp.exp(steps), shape[dim] // blocks).reshape((-1,) + (1,) * (len(shape) - dim - 1))

    level = one(*split[0])
    for cut in split[1:]:
        level = level * one(*cut)
    return level


def noise(stream_key, extent, deviation, limit, split=(), kind=jnp.bfloat16):
    drawn = jax.random.normal(stream_key, extent, jnp.float32) * deviation
    if len(split) > 0:
        drawn = levels(stream_key, extent, split, -0.22, 0.18) * drawn
    return jnp.clip(drawn, min=-limit, max=limit).astype(kind)


def setup_inputs(seed: int = 0) -> dict:
    key_of = jax.random.split(jax.random.key(seed), 6)
    right_side = noise(key_of[0], (NODES, NODES, NODES, ELEMENTS), 1.0, 8.0, ((3, 32),), jnp.float32)
    stretch = jnp.clip(jnp.exp(math.log(3.0) - 2.3025851 * jax.random.uniform(key_of[1], (3, ELEMENTS), jnp.float32) ** levels(key_of[1], (3, ELEMENTS), ((1, 32),), -0.2, 0.2)), 0.3, 3.0)
    mass_term = jnp.clip(jnp.exp(math.log(2.0) - 1.3862944 * jax.random.uniform(key_of[2], (ELEMENTS,), jnp.float32) ** levels(key_of[2], (ELEMENTS,), ((0, 32),), -0.2, 0.2)), 0.5, 2.0)
    slot_position = draw_slot_position(jax.random.fold_in(key_of[5], 71), 0)
    coarse_group = draw_coarse_group(jax.random.fold_in(key_of[5], 71), 0)
    return {"right_side": right_side, "stretch": stretch, "mass_term": mass_term, "slot_position": slot_position, "coarse_group": coarse_group}


relax_factor = 0.35

def leading(values, axis, amount):
    return lax.slice_in_dim(values, 0, amount, axis=axis)

def trailing(values, axis, amount):
    size = values.shape[axis]
    return lax.slice_in_dim(values, size - amount, size, axis=axis)

def extend_axis(values, node_axis, elem_axis):
    top_layer = trailing(values, node_axis, 1)
    bottom = leading(values, node_axis, 1)
    elements = values.shape[elem_axis]
    empty = jnp.zeros_like(trailing(top_layer, elem_axis, 1))
    below_layer = jnp.concatenate([empty, leading(top_layer, elem_axis, elements - 1)], axis=elem_axis)
    above_layer = jnp.concatenate([trailing(bottom, elem_axis, elements - 1), empty], axis=elem_axis)
    return jnp.concatenate([below_layer, values, above_layer], axis=node_axis)

def narrow(extended, node_axis, elem_axis):
    size = extended.shape[node_axis]
    interior = lax.slice_in_dim(extended, 1, size - 1, axis=node_axis)
    lower_rim = leading(extended, node_axis, 1)
    upper_rim = trailing(extended, node_axis, 1)
    elements = extended.shape[elem_axis]
    empty = jnp.zeros_like(trailing(lower_rim, elem_axis, 1))
    add_top = jnp.concatenate([trailing(lower_rim, elem_axis, elements - 1), empty], axis=elem_axis)
    add_bottom = jnp.concatenate([empty, leading(upper_rim, elem_axis, elements - 1)], axis=elem_axis)
    inner_size = interior.shape[node_axis]
    first_layer = leading(interior, node_axis, 1) + add_bottom
    last_layer = trailing(interior, node_axis, 1) + add_top
    middle = lax.slice_in_dim(interior, 1, inner_size - 1, axis=node_axis)
    return jnp.concatenate([first_layer, middle, last_layer], axis=node_axis)

def tables(points):
    order = points + 2
    column = jnp.arange(order).astype(jnp.float32) + 1.0
    sines = jnp.sqrt(2.0 / (order + 1.0)) * jnp.sin(jnp.pi * column[:, None] * column[None, :] / (order + 1.0))
    eigen_values = 2.0 - 2.0 * jnp.cos(jnp.pi * column / (order + 1.0))
    return (sines, eigen_values)

def local_solve(extended, coeffs, mass_grid):
    sines, eigen_values = tables(extended.shape[0] - 2)
    highest = lax.Precision.HIGHEST
    spectral = jnp.einsum('ip,pqrabc->iqrabc', sines, extended, precision=highest)
    spectral = jnp.einsum('jq,iqrabc->ijrabc', sines, spectral, precision=highest)
    spectral = jnp.einsum('kr,ijrabc->ijkabc', sines, spectral, precision=highest)
    lam_i = eigen_values[:, None, None, None, None, None]
    lam_j = eigen_values[None, :, None, None, None, None]
    lam_k = eigen_values[None, None, :, None, None, None]
    denominator = coeffs[0][None, None, None] * lam_i + coeffs[1][None, None, None] * lam_j + coeffs[2][None, None, None] * lam_k + mass_grid[None, None, None]
    spectral = spectral / denominator
    spectral = jnp.einsum('ip,pqrabc->iqrabc', sines, spectral, precision=highest)
    spectral = jnp.einsum('jq,iqrabc->ijrabc', sines, spectral, precision=highest)
    return jnp.einsum('kr,ijrabc->ijkabc', sines, spectral, precision=highest)

def operate(extended, coeffs, mass_grid):
    centre = extended[1:-1, 1:-1, 1:-1]
    lap_x = 2.0 * centre - extended[2:, 1:-1, 1:-1] - extended[:-2, 1:-1, 1:-1]
    lap_y = 2.0 * centre - extended[1:-1, 2:, 1:-1] - extended[1:-1, :-2, 1:-1]
    lap_z = 2.0 * centre - extended[1:-1, 1:-1, 2:] - extended[1:-1, 1:-1, :-2]
    return coeffs[0] * lap_x + coeffs[1] * lap_y + coeffs[2] * lap_z + mass_grid * centre

def extend_all(values):
    return extend_axis(extend_axis(extend_axis(values, 0, 3), 1, 4), 2, 5)

def fold_all(extended):
    return narrow(narrow(narrow(extended, 2, 5), 1, 4), 0, 3)

def reference(right_side, stretch, mass_term, slot_position, coarse_group):
    grid_x = EX * N_SX
    grid_y = EY * N_SY
    element = jnp.arange(ELEMENTS, dtype=jnp.int32)
    device = element // E_DEV
    row_index = device // N_SY
    col_index = device % N_SY
    along_x = slot_position // (EY * EZ)
    along_y = slot_position // EZ % EY
    along_z = slot_position % EZ
    flat_index = (((row_index * EX + along_x) * grid_y + col_index * EY + along_y) * EZ + along_z).astype(jnp.int32)
    grid_shape = (NODES, NODES, NODES, grid_x, grid_y, EZ)
    source = jnp.zeros((NODES, NODES, NODES, ELEMENTS), jnp.float32).at[:, :, :, flat_index].set(right_side).reshape(grid_shape)
    coeffs = jnp.zeros((3, ELEMENTS), jnp.float32).at[:, flat_index].set(stretch).reshape(3, grid_x, grid_y, EZ)
    mass_grid = jnp.zeros((ELEMENTS,), jnp.float32).at[flat_index].set(mass_term).reshape(grid_x, grid_y, EZ)
    solution = jnp.zeros_like(source)
    residual = source
    for sweep in range(SWEEPS):
        correction = fold_all(local_solve(extend_all(residual), coeffs, mass_grid))
        solution = solution + relax_factor * correction
        residual = source - operate(extend_all(solution), coeffs, mass_grid)
    flat_shape = (NODES, NODES, NODES, ELEMENTS)
    smoothed = jnp.take(solution.reshape(flat_shape), flat_index, axis=3)
    fine_residual = jnp.take(residual.reshape(flat_shape), flat_index, axis=3)
    position = jnp.arange(NODES).astype(jnp.float32) / (NODES - 1.0)
    linear_weights = jnp.stack([1.0 - position, position])
    highest = lax.Precision.HIGHEST
    moments = jnp.einsum('xp,yq,zr,pqre->xyze', linear_weights, linear_weights, linear_weights, fine_residual, precision=highest).reshape(8, ELEMENTS)
    coarse_rhs = jax.ops.segment_sum(moments.T, coarse_group, num_segments=GROUPS).T
    return (smoothed, fine_residual, coarse_rhs)
```

```python
import numpy as np
import jax
import jax.numpy as jnp
from jax import lax
from jax.experimental import pallas as pl
from jax.experimental.pallas import tpu as pltpu
from jax.sharding import PartitionSpec as P

NODES = 8
EY = 2
EZ = 128
GRP_DEV = 16
RELAX = 0.35
ORDER = NODES + 2
F32 = jnp.float32
BF16 = jnp.bfloat16
MESH = pl.DeviceIdType.MESH

WY = EY * NODES + 4
NQ = ORDER * WY
NP = ORDER * ORDER

_m = np.arange(1, ORDER + 1, dtype=np.float64)
_S = np.sqrt(2.0 / (ORDER + 1)) * np.sin(np.pi * np.outer(_m, _m) / (ORDER + 1))
_LAM = 2.0 - 2.0 * np.cos(np.pi * _m / (ORDER + 1))
_C = _S / _S[0:1, :]
_HALF = ORDER // 2

DIRS = [(dx, dy) for dx in (-1, 0, 1) for dy in (-1, 0, 1) if (dx, dy) != (0, 0)]
ND = len(DIRS)


def forward(g):
    a = [g[i] + g[ORDER - 1 - i] for i in range(_HALF)]
    b = [g[i] - g[ORDER - 1 - i] for i in range(_HALF)]
    out = []
    for k in range(ORDER):
        part = a if k % 2 == 0 else b
        total = part[0]
        for i in range(1, _HALF):
            total = total + float(_C[i, k]) * part[i]
        out.append(total)
    return out


def backward(v):
    low, high = [], []
    for i in range(_HALF):
        sums = []
        for parity in (0, 1):
            total = None
            for k in range(parity, ORDER, 2):
                term = v[k] if i == 0 else float(_C[i, k]) * v[k]
                total = term if total is None else total + term
            sums.append(total)
        low.append(sums[0] + sums[1])
        high.append(sums[0] - sums[1])
    return low + high[::-1]


def split3(x):
    hi = x.astype(BF16)
    rest = x - hi.astype(F32)
    mid = rest.astype(BF16)
    low = (rest - mid.astype(F32)).astype(BF16)
    return hi, mid, low


def exact_dot(x, table, contract):
    dims = (((1,), (contract,)), ((), ()))
    parts = [lax.dot_general(s, table, dims, preferred_element_type=F32) for s in split3(x)]
    return parts[0] + (parts[1] + parts[2])


def span_send(d, layers, size, base):
    if d > 0:
        return base + size - (layers - 1), layers
    if d < 0:
        return base - 1, layers
    return base - 1, size + 2


def span_recv(d, layers, size, base):
    if d > 0:
        return base - (layers - 1), layers
    if d < 0:
        return base + size - 1, layers
    return base - 1, size + 2


def slab_shape(d, layers):
    return (
        span_send(d[0], layers, NODES, 1)[1],
        span_send(d[1], layers, EY * NODES, 2)[1],
        NODES,
        EZ,
    )


def make_kernel(n_sx, n_sy):
    def kernel(*refs):
        (rs, stretch, mass, slot, group, tables, sm_out, fr_out, co_out) = refs[:9]
        (perm, cb, cc, cn, cf, rt, F, U, PA, PB, zs, ys, ro, mo, sb, rb) = refs[9:25]
        bufs2 = refs[25 : 25 + ND]
        bufs3 = refs[25 + ND : 25 + 2 * ND]
        (s1, r1, sc, rc, s2, r2, s3, r3, s4, r4) = refs[25 + 2 * ND :]
        i = lax.axis_index("sx")
        j = lax.axis_index("sy")

        def exists(dx, dy):
            ok = None
            for pos, d, size in ((i, dx, n_sx), (j, dy, n_sy)):
                cond = pos < size - 1 if d > 0 else (pos > 0 if d < 0 else None)
                if cond is not None:
                    ok = cond if ok is None else jnp.logical_and(ok, cond)
            return ok

        lane = lax.broadcasted_iota(jnp.int32, (8, EZ), 1)
        sub = lax.broadcasted_iota(jnp.int32, (8, EZ), 0)
        zero_tile = jnp.zeros((8, EZ), F32)

        def from_below(v):
            return jnp.where(lane == 0, 0.0, pltpu.roll(v, 1, 1))

        def from_above(v):
            return jnp.where(lane == EZ - 1, 0.0, pltpu.roll(v, EZ - 1, 1))

        for y in range(WY):
            F[0, y] = zero_tile
            F[ORDER - 1, y] = zero_tile
        for x in range(1, ORDER - 1):
            for y in (0, 1, WY - 2, WY - 1):
                F[x, y] = zero_tile
        for n in range(ND):
            cn[n] = zero_tile

        barrier = pltpu.get_barrier_semaphore()
        count = n_sy - 1
        for d in range(1, n_sy):
            pl.semaphore_signal(
                barrier, inc=1, device_id=(i, lax.rem(j + d, n_sy)), device_id_type=MESH
            )
        for dx, dy in DIRS:
            if dx == 0:
                continue
            ok = exists(dx, dy)
            count = count + ok.astype(jnp.int32)

            @pl.when(ok)
            def _():
                pl.semaphore_signal(
                    barrier, inc=1, device_id=(i + dx, j + dy), device_id_type=MESH
                )

        positions = lax.broadcasted_iota(jnp.int32, (EY * EZ, EY * EZ), 0)
        perm[...] = jnp.where(positions == slot[...], 1.0, 0.0).astype(BF16)
        table = perm[...]
        cb[...] = jnp.zeros_like(cb)
        cb[0:3, :] = stretch[...]
        cb[3:4, :] = mass[...]
        ordered = exact_dot(cb[...], table, 1)
        cc[0:4, :] = ordered[0:4, 0:EZ]
        cc[4:8, :] = ordered[0:4, EZ : 2 * EZ]
        Fr = F.reshape(NQ * 8, EZ)
        Ur = U.reshape((ORDER + 2) * WY * 8, EZ)
        for x in range(NODES):
            got = exact_dot(rs[x * 64 : x * 64 + 64, :], perm[...], 1)
            start = ((x + 1) * WY + 2) * 8
            Fr[start : start + 64, :] = got[:, 0:EZ]
            Fr[start + 64 : start + 128, :] = got[:, EZ : 2 * EZ]

        pl.semaphore_wait(barrier, count)

        def edge(d, size, base, sending):
            if d > 0:
                return pl.ds(base + size - 1 if sending else base - 1, 1)
            if d < 0:
                return pl.ds(base if sending else base + size, 1)
            return pl.ds(base, size)

        def copies1(n):
            dx, dy = DIRS[n]
            target = (i + dx, j + dy)
            field = pltpu.make_async_remote_copy(
                src_ref=F.at[edge(dx, NODES, 1, True), edge(dy, EY * NODES, 2, True)],
                dst_ref=F.at[edge(dx, NODES, 1, False), edge(dy, EY * NODES, 2, False)],
                send_sem=s1.at[n],
                recv_sem=r1.at[n],
                device_id=target,
                device_id_type=MESH,
            )
            coeff = pltpu.make_async_remote_copy(
                src_ref=cc,
                dst_ref=cn.at[n],
                send_sem=sc.at[n],
                recv_sem=rc.at[n],
                device_id=target,
                device_id_type=MESH,
            )
            return field, coeff

        def slab_copy(n, source, bufs, layers, ssem, rsem):
            dx, dy = DIRS[n]
            x0, nx = span_send(dx, layers, NODES, 1)
            y0, ny = span_send(dy, layers, EY * NODES, 2)
            return [
                pltpu.make_async_remote_copy(
                    src_ref=source.at[pl.ds(x0, nx), pl.ds(y0, ny)],
                    dst_ref=bufs[n],
                    send_sem=ssem.at[n],
                    recv_sem=rsem.at[n],
                    device_id=(i + dx, j + dy),
                    device_id_type=MESH,
                )
            ]

        def start_all(make):
            for n, (dx, dy) in enumerate(DIRS):

                @pl.when(exists(dx, dy))
                def _():
                    for copy in make(n):
                        copy.start()

        def wait_sends(make):
            for n, (dx, dy) in enumerate(DIRS):

                @pl.when(exists(dx, dy))
                def _():
                    for copy in make(n):
                        copy.wait_send()

        start_all(copies1)

        @pl.loop(0, 2 * NP // 8)
        def _(t):
            row = pl.multiple_of(t * 8, 8)
            upper = row + sub >= NP
            part = [jnp.where(upper, cc[4 + c : 5 + c, :], cc[c : c + 1, :]) for c in range(4)]
            scale = tables[pl.ds(4 * NP + row, 8), :]
            base = (
                part[1] * tables[pl.ds(row, 8), :]
                + part[2] * tables[pl.ds(2 * NP + row, 8), :]
                + part[3]
            )
            for k in range(ORDER):
                rt[pl.ds(pl.multiple_of(t * (8 * ORDER) + 8 * k, 8), 8), :] = (
                    scale * float(_S[0, k] ** 2)
                ) / (base + part[0] * float(_LAM[k]))

        for n, (dx, dy) in enumerate(DIRS):

            @pl.when(exists(-dx, -dy))
            def _():
                for copy in copies1(n):
                    copy.wait_recv()

        for c in range(4):

            def row_of(dx, dy, e):
                if (dx, dy) == (0, 0):
                    return cc[4 * e + c : 4 * e + c + 1, :]
                return cn[DIRS.index((-dx, -dy)), 4 * e + c : 4 * e + c + 1, :]

            for xs, dx in (((0,), -1), (range(1, ORDER - 1), 0), ((ORDER - 1,), 1)):
                first = row_of(dx, -1, 1)
                last = row_of(dx, 1, 0)
                low = jnp.broadcast_to(row_of(dx, 0, 0), (8, EZ))
                high = jnp.broadcast_to(row_of(dx, 0, 1), (8, EZ))
                for x in xs:
                    at = c * NQ + x * WY
                    cf[at : at + 1, :] = jnp.zeros((1, EZ), F32)
                    cf[at + 1 : at + 2, :] = first
                    cf[at + 2 : at + 10, :] = low
                    cf[at + 10 : at + 18, :] = high
                    cf[at + 18 : at + 19, :] = last
                    cf[at + 19 : at + 20, :] = jnp.zeros((1, EZ), F32)

        def load_z(ref, row):
            return [ref[pl.ds(row * 8 + z, 8, stride=8), :] for z in range(NODES)]

        def residual(f, q, coef):
            u = load_z(Ur, q + WY)
            xa, xb = load_z(Ur, q), load_z(Ur, q + 2 * WY)
            ya, yb = load_z(Ur, q + WY - 1), load_z(Ur, q + WY + 1)
            line = [from_below(u[-1])] + u + [from_above(u[0])]
            cx, cy, cz, m = coef
            diag = 2.0 * (cx + cy + cz) + m
            return [
                f[z]
                - (
                    diag * u[z]
                    - cx * (xa[z] + xb[z])
                    - cy * (ya[z] + yb[z])
                    - cz * (line[z] + line[z + 2])
                )
                for z in range(NODES)
            ]

        def solve(first, out):
            outr = out.reshape(NQ * 8, EZ)

            @pl.loop(0, NQ // 8)
            def _(t):
                q = pl.multiple_of(t * 8, 8)
                g = load_z(Fr, q)
                if not first:
                    g = residual(g, q, [cf[pl.ds(c * NQ + q, 8), :] for c in range(4)])
                v = forward([from_below(g[-1])] + g + [from_above(g[0])])
                for k in range(ORDER):
                    zs[pl.ds(pl.multiple_of(k * NQ + q, 8), 8), :] = v[k]

            @pl.loop(0, 13)
            def _(t):
                p = jnp.minimum(t * 8, NP - 8)
                rows = [zs[pl.ds(p * WY + 1 + y, 8, stride=WY), :] for y in range(WY - 2)]
                for e in range(EY):
                    v = forward(rows[8 * e : 8 * e + ORDER])
                    for k in range(ORDER):
                        ys[pl.ds((e * ORDER + k) * NP + p, 8), :] = v[k]

            @pl.loop(0, 2 * NP // 8)
            def _(t):
                row = t * (8 * ORDER)
                v = forward([ys[pl.ds(row + x, 8, stride=ORDER), :] for x in range(ORDER)])
                v = [
                    v[k] * rt[pl.ds(pl.multiple_of(row + 8 * k, 8), 8), :] for k in range(ORDER)
                ]
                v = backward(v)
                for x in range(ORDER):
                    ys[pl.ds(row + x, 8, stride=ORDER), :] = v[x]

            @pl.loop(0, 13)
            def _(t):
                p = jnp.minimum(t * 8, NP - 8)
                a = backward([ys[pl.ds(k * NP + p, 8), :] for k in range(ORDER)])
                b = backward([ys[pl.ds((ORDER + k) * NP + p, 8), :] for k in range(ORDER)])
                rows = a[:8] + [a[8] + b[0], a[9] + b[1]] + b[2:]
                for y in range(WY - 2):
                    zs[pl.ds(p * WY + 1 + y, 8, stride=WY), :] = rows[y]

            @pl.loop(0, NQ // 8)
            def _(t):
                q = pl.multiple_of(t * 8, 8)
                v = backward([zs[pl.ds(pl.multiple_of(k * NQ + q, 8), 8), :] for k in range(ORDER)])
                body = v[1:-1]
                body[0] = body[0] + from_below(v[-1])
                body[-1] = body[-1] + from_above(v[0])
                for z in range(NODES):
                    outr[pl.ds(q * 8 + z, 8, stride=8), :] = body[z]

            for edge_x, ok in ((0, i > 0), (ORDER - 1, i < n_sx - 1)):

                @pl.when(jnp.logical_not(ok))
                def _():
                    for y in range(WY):
                        out[edge_x, y] = zero_tile

            for edge_y, ok in ((1, j > 0), (WY - 2, j < n_sy - 1)):

                @pl.when(jnp.logical_not(ok))
                def _():
                    for x in range(ORDER):
                        out[x, edge_y] = zero_tile

        def gather(n, make, bufs, layers):
            dx, dy = DIRS[n]

            @pl.when(exists(-dx, -dy))
            def _():
                for copy in make(n):
                    copy.wait_recv()
                x0, nx = span_recv(dx, layers, NODES, 2)
                y0, ny = span_recv(dy, layers, EY * NODES, 2)

                @pl.loop(0, nx)
                def _(x):
                    U[pl.ds(x0 + x, 1), pl.ds(y0, ny)] = (
                        U[pl.ds(x0 + x, 1), pl.ds(y0, ny)] + bufs[n][pl.ds(x, 1)]
                    )

        inner = pl.ds(1, WY - 2)

        @pl.loop(0, ORDER + 2)
        def _(x):
            U[pl.ds(x, 1)] = jnp.zeros((1, WY, 8, EZ), F32)

        solve(True, PA)
        make2 = lambda n: slab_copy(n, PA, bufs2, 3, s2, r2)
        start_all(make2)

        @pl.loop(0, ORDER)
        def _(x):
            U[pl.ds(x + 1, 1), inner] = PA[pl.ds(x, 1), inner]

        for n in range(ND):
            gather(n, make2, bufs2, 3)

        solve(False, PB)
        make3 = lambda n: slab_copy(n, PB, bufs3, 2, s3, r3)
        start_all(make3)

        @pl.loop(0, ORDER)
        def _(x):
            U[pl.ds(x + 1, 1), inner] = U[pl.ds(x + 1, 1), inner] + PB[pl.ds(x, 1), inner]

        for n in range(ND):
            gather(n, make3, bufs3, 2)

        weights = [((NODES - 1 - t) / (NODES - 1), t / (NODES - 1)) for t in range(NODES)]
        coefs = [
            [jnp.broadcast_to(cc[4 * h + c : 4 * h + c + 1, :], (8, EZ)) for c in range(4)]
            for h in range(EY)
        ]

        def last(x, carry):
            wx = x.astype(F32) * (1.0 / (NODES - 1))
            carry = list(carry)
            for h in range(EY):
                q = (x + 1) * WY + 2 + 8 * h
                r = residual(load_z(Fr, q), q, coefs[h])
                for z in range(NODES):
                    ro[pl.ds((x * 16 + 8 * h) * 8 + z, 8, stride=8), :] = r[z]
                for c in range(2):
                    total = None
                    for z in range(NODES):
                        if weights[z][c] == 0.0:
                            continue
                        term = weights[z][c] * r[z]
                        total = term if total is None else total + term
                    carry[4 * h + c] = carry[4 * h + c] + (1.0 - wx) * total
                    carry[4 * h + 2 + c] = carry[4 * h + 2 + c] + wx * total
            return tuple(carry)

        acc = lax.fori_loop(0, NODES, last, tuple([zero_tile] * 8))
        wy1 = sub.astype(F32) * (1.0 / (NODES - 1))
        for h in range(EY):
            for a in range(2):
                for b in range(2):
                    for c in range(2):
                        w = wy1 if b else 1.0 - wy1
                        row = jnp.sum(acc[4 * h + 2 * a + c] * w, axis=0, keepdims=True)
                        v = 4 * a + 2 * b + c
                        mo[v : v + 1, EZ * h : EZ * (h + 1)] = row
        moments = exact_dot(mo[...], perm[...], 0)
        groups = GRP_DEV * n_sy
        column = group[...] - i * groups
        onehot = jnp.where(
            lax.broadcasted_iota(jnp.int32, (groups, EY * EZ), 0) == column, 1.0, 0.0
        ).astype(BF16)
        partial = exact_dot(moments, onehot, 1)
        per = EZ // GRP_DEV
        for d in range(n_sy):
            block = partial[:, (d // per) * EZ : (d // per + 1) * EZ]
            shift = (d % per) * GRP_DEV
            sb[d] = block if shift == 0 else pltpu.roll(block, EZ - shift, 1)

        def copy4(d):
            dest = lax.rem(j + d, n_sy)
            return pltpu.make_async_remote_copy(
                src_ref=sb.at[dest],
                dst_ref=rb.at[d - 1],
                send_sem=s4.at[d - 1],
                recv_sem=r4.at[d - 1],
                device_id=(i, dest),
                device_id_type=MESH,
            )

        for d in range(1, n_sy):
            copy4(d).start()

        @pl.loop(0, NODES)
        def _(x):
            start = pl.multiple_of(((x + 2) * WY + 2) * 8, 8)
            rows = pl.ds(pl.multiple_of(x * 64, 64), 64)
            u = jnp.concatenate([Ur[pl.ds(start, 64), :], Ur[pl.ds(start + 64, 64), :]], axis=1)
            sm_out[rows, :] = exact_dot(u, perm[...], 0)
            at = pl.multiple_of(x * 128, 128)
            r = jnp.concatenate([ro[pl.ds(at, 64), :], ro[pl.ds(at + 64, 64), :]], axis=1)
            fr_out[rows, :] = exact_dot(r, perm[...], 0)

        wait_sends(copies1)
        wait_sends(make2)
        wait_sends(make3)
        total = sb[j]
        for d in range(1, n_sy):
            copy4(d).wait()
            total = total + rb[d - 1]
        co_out[...] = total[:, 0:GRP_DEV]

    return kernel


def solution(mesh):
    n_sx, n_sy = mesh.shape["sx"], mesh.shape["sy"]
    lam_l = np.tile(np.repeat(_LAM, ORDER), 2)
    lam_k = np.tile(_LAM, 2 * ORDER)
    s0 = _S[0] ** 2
    scale = RELAX * np.tile(np.repeat(s0, ORDER), 2) * np.tile(s0, 2 * ORDER)
    column = np.concatenate([lam_l, lam_k, scale]).astype(np.float32)

    def on_device(right_side, stretch, mass_term, slot_position, coarse_group):
        elements = right_side.shape[3]
        tables = jnp.broadcast_to(jnp.asarray(column)[:, None], (column.size, EZ))
        vmem = pl.BlockSpec(memory_space=pltpu.VMEM)
        V = lambda *shape: pltpu.VMEM(shape, F32)
        dma = lambda n: pltpu.SemaphoreType.DMA((n,))
        points = NODES**3
        scratch = [
            pltpu.VMEM((elements, elements), BF16),
            V(8, elements),
            V(8, EZ),
            V(ND, 8, EZ),
            V(4 * NQ, EZ),
            V(2 * NP * ORDER, EZ),
            V(ORDER, WY, 8, EZ),
            V(ORDER + 2, WY, 8, EZ),
            V(ORDER, WY, 8, EZ),
            V(ORDER, WY, 8, EZ),
            V(ORDER * NQ, EZ),
            V(2 * NP * ORDER, EZ),
            V(2 * points, EZ),
            V(8, elements),
            V(n_sy, 8, EZ),
            V(max(n_sy - 1, 1), 8, EZ),
        ]
        scratch += [V(*slab_shape(d, 3)) for d in DIRS]
        scratch += [V(*slab_shape(d, 2)) for d in DIRS]
        scratch += [dma(ND)] * 8 + [dma(max(n_sy - 1, 1))] * 2
        smoothed, fine, coarse = pl.pallas_call(
            make_kernel(n_sx, n_sy),
            out_shape=(
                jax.ShapeDtypeStruct((points, elements), F32),
                jax.ShapeDtypeStruct((points, elements), F32),
                jax.ShapeDtypeStruct((8, GRP_DEV), F32),
            ),
            in_specs=[vmem] * 6,
            out_specs=(vmem, vmem, vmem),
            scratch_shapes=scratch,
            compiler_params=pltpu.CompilerParams(
                collective_id=0, has_side_effects=True, vmem_limit_bytes=48 * 1024 * 1024
            ),
        )(
            right_side.reshape(points, elements),
            stretch,
            mass_term.reshape(1, elements),
            slot_position.reshape(1, elements),
            coarse_group.reshape(1, elements),
            tables,
        )
        shape = right_side.shape
        return smoothed.reshape(shape), fine.reshape(shape), coarse

    split = ("sx", "sy")
    field = P(None, None, None, split)
    return jax.shard_map(
        on_device,
        mesh=mesh,
        in_specs=(field, P(None, split), P(split), P(split), P(split)),
        out_specs=(field, field, P(None, split)),
        check_vma=False,
    )
```

```python
import numpy as np
import jax
import jax.numpy as jnp
from jax import lax
from jax.experimental import pallas as pl
from jax.experimental.pallas import tpu as pltpu
from jax.sharding import PartitionSpec as P

NODES = 8
EY = 2
EZ = 128
GRP_DEV = 16
RELAX = 0.35
ORDER = NODES + 2
F32 = jnp.float32
BF16 = jnp.bfloat16
MESH = pl.DeviceIdType.MESH

WY = EY * NODES + 4
LX = NODES * WY
NQ = ORDER * WY
NP = ORDER * ORDER
NT = 13
TY = EY * NODES

_m = np.arange(1, ORDER + 1, dtype=np.float64)
_S = np.sqrt(2.0 / (ORDER + 1)) * np.sin(np.pi * np.outer(_m, _m) / (ORDER + 1))
_LAM = 2.0 - 2.0 * np.cos(np.pi * _m / (ORDER + 1))
_C = _S / _S[0:1, :]
_HALF = ORDER // 2

DIRS = [(dx, dy) for dx in (-1, 0, 1) for dy in (-1, 0, 1) if (dx, dy) != (0, 0)]
ND = len(DIRS)


def forward(g):
    a = [g[i] + g[ORDER - 1 - i] for i in range(_HALF)]
    b = [g[i] - g[ORDER - 1 - i] for i in range(_HALF)]
    out = []
    for k in range(ORDER):
        part = a if k % 2 == 0 else b
        total = part[0]
        for i in range(1, _HALF):
            total = total + float(_C[i, k]) * part[i]
        out.append(total)
    return out


def backward(v):
    low, high = [], []
    for i in range(_HALF):
        sums = []
        for parity in (0, 1):
            total = None
            for k in range(parity, ORDER, 2):
                term = v[k] if i == 0 else float(_C[i, k]) * v[k]
                total = term if total is None else total + term
            sums.append(total)
        low.append(sums[0] + sums[1])
        high.append(sums[0] - sums[1])
    return low + high[::-1]


def split3(x):
    hi = x.astype(BF16)
    rest = x - hi.astype(F32)
    mid = rest.astype(BF16)
    low = (rest - mid.astype(F32)).astype(BF16)
    return hi, mid, low


def exact_dot(x, table, contract):
    dims = (((1,), (contract,)), ((), ()))
    parts = [lax.dot_general(s, table, dims, preferred_element_type=F32) for s in split3(x)]
    return parts[0] + (parts[1] + parts[2])


def edge_range(d, size, layers):
    if d > 0:
        return range(size - layers + 1, size + 1)
    return range(-1, layers - 1)


def slab_messages(layers, early):
    out = []
    for group, dy in ((early, 1 if early else -1), (1 - early, -1 if early else 1)):
        for dx in (0, -1, 1):
            xs = range(-1, NODES + 1) if dx == 0 else edge_range(dx, NODES, layers)
            ys = edge_range(dy, TY, layers)
            far_x = None if dx == 0 else (xs[0] if dx > 0 else xs[-1])
            far_y = ys[0] if dy > 0 else ys[-1]
            tiles = [("v", x, y) for y in ys for x in xs if (x, y) != (far_x, far_y)]
            out.append((dx, dy, group, tiles))
        for dx in (-1, 1):
            xs = edge_range(dx, NODES, layers)
            start = 9 if group else -1
            tiles = [("h", x, z, start) for x in xs for z in range(NODES)]
            if group != early:
                tiles += [("v", x, y) for x in xs for y in (7, 8)]
            out.append((dx, 0, group, tiles))
    return out


def field_messages():
    out = []
    for dx, dy in DIRS:
        xs = range(NODES) if dx == 0 else ((NODES - 1,) if dx > 0 else (0,))
        if dy == 0:
            tiles = [("h", x, z, y) for x in xs for z in range(NODES) for y in (0, 8)]
        else:
            tiles = [("v", x, TY - 1 if dy > 0 else 0) for x in xs]
        out.append((dx, dy, 0, tiles))
    return out


ROUNDS = (field_messages(), slab_messages(3, 1), slab_messages(2, 0))


def message_size(message):
    return len(message[3]) + (1 if message in ROUNDS[0] else 0)


def tile_at(tile, shift_x, shift_y):
    if tile[0] == "v":
        return pl.ds((tile[1] + shift_x) * LX + tile[2] + shift_y, 8, stride=WY)
    return pl.ds(((tile[1] + shift_x) * NODES + tile[2]) * WY + tile[3] + shift_y, 8)


def make_kernel(n_sx, n_sy):
    def kernel(*refs):
        (rs, stretch, mass, slot, group, tables, sm_out, fr_out, co_out) = refs[:9]
        (perm, cb, cc, cn, cf, rt, F, U, PA, zs, zi, ys, yt, ov, ro, mo, sb, rb) = refs[9:27]
        at = 27
        rounds = []
        for messages in ROUNDS:
            n = len(messages)
            rounds.append(
                (messages, refs[at : at + n], refs[at + n : at + 2 * n]) + refs[at + 2 * n : at + 2 * n + 2]
            )
            at += 2 * n + 2
        s4, r4 = refs[at : at + 2]
        i = lax.axis_index("sx")
        j = lax.axis_index("sy")

        def exists(dx, dy):
            ok = None
            for pos, d, size in ((i, dx, n_sx), (j, dy, n_sy)):
                cond = pos < size - 1 if d > 0 else (pos > 0 if d < 0 else None)
                if cond is not None:
                    ok = cond if ok is None else jnp.logical_and(ok, cond)
            return ok

        lane = lax.broadcasted_iota(jnp.int32, (8, EZ), 1)
        sub = lax.broadcasted_iota(jnp.int32, (8, EZ), 0)
        zero_tile = jnp.zeros((8, EZ), F32)

        def from_below(v):
            return jnp.where(lane == 0, 0.0, pltpu.roll(v, 1, 1))

        def from_above(v):
            return jnp.where(lane == EZ - 1, 0.0, pltpu.roll(v, EZ - 1, 1))

        barrier = pltpu.get_barrier_semaphore()
        count = n_sy - 1
        for d in range(1, n_sy):
            pl.semaphore_signal(
                barrier, inc=1, device_id=(i, lax.rem(j + d, n_sy)), device_id_type=MESH
            )
        for dx, dy in DIRS:
            if dx == 0:
                continue
            ok = exists(dx, dy)
            count = count + ok.astype(jnp.int32)

            @pl.when(ok)
            def _():
                pl.semaphore_signal(
                    barrier, inc=1, device_id=(i + dx, j + dy), device_id_type=MESH
                )

        for n in range(ND):
            cn[n] = zero_tile

        positions = lax.broadcasted_iota(jnp.int32, (EY * EZ, EY * EZ), 0)
        perm[...] = jnp.where(positions == slot[...], 1.0, 0.0).astype(BF16)
        cb[...] = jnp.zeros_like(cb)
        cb[0:3, :] = stretch[...]
        cb[3:4, :] = mass[...]
        ordered = exact_dot(cb[...], perm[...], 1)
        cc[0:4, :] = ordered[0:4, 0:EZ]
        cc[4:8, :] = ordered[0:4, EZ : 2 * EZ]
        for x in range(NODES):
            got = exact_dot(rs[x * 64 : x * 64 + 64, :], perm[...], 1)
            for y in range(TY):
                part = got[8 * (y % 8) : 8 * (y % 8) + 8, EZ * (y // 8) : EZ * (y // 8 + 1)]
                F[tile_at(("v", x, y), 1, 2), :] = part

        for x in range(ORDER):
            for y in (range(WY) if x in (0, ORDER - 1) else (0, 1, WY - 2, WY - 1)):
                F[pl.ds(x * LX + y, 8, stride=WY), :] = zero_tile
            for y in (0, WY - 1):
                PA[pl.ds(x * LX + y, 8, stride=WY), :] = zero_tile

        pl.semaphore_wait(barrier, count)

        def copy_of(r, n):
            messages, send, recv, ssem, rsem = rounds[r]
            dx, dy = messages[n][:2]
            return pltpu.make_async_remote_copy(
                src_ref=send[n],
                dst_ref=recv[n],
                send_sem=ssem.at[n],
                recv_sem=rsem.at[n],
                device_id=(i + dx, j + dy),
                device_id_type=MESH,
            )

        def post(r, source, wanted):
            messages, send = rounds[r][:2]
            for n, (dx, dy, g, tiles) in enumerate(messages):
                if not wanted(dx, dy, g):
                    continue

                @pl.when(exists(dx, dy))
                def _():
                    for k, tile in enumerate(tiles):
                        send[n][8 * k : 8 * k + 8, :] = source[tile_at(tile, 1, 2), :]
                    if r == 0:
                        send[n][8 * len(tiles) : 8 * len(tiles) + 8, :] = cc[...]
                    copy_of(r, n).start()

        def collect(r, wanted):
            messages, send, recv = rounds[r][:3]
            for n, (dx, dy, g, tiles) in enumerate(messages):
                if not wanted(dx, dy, g):
                    continue

                @pl.when(exists(-dx, -dy))
                def _():
                    copy_of(r, n).wait_recv()
                    for k, tile in enumerate(tiles):
                        got = recv[n][8 * k : 8 * k + 8, :]
                        if r == 0:
                            F[tile_at(tile, 1 - NODES * dx, 2 - TY * dy), :] = got
                        else:
                            here = tile_at(tile, 2 - NODES * dx, 2 - TY * dy)
                            U[here, :] = U[here, :] + got
                    if r == 0:
                        cn[n] = recv[n][8 * len(tiles) : 8 * len(tiles) + 8, :]

        everything = lambda dx, dy, g: True
        post(0, F, everything)

        for e in range(EY):
            part = [jnp.broadcast_to(cc[4 * e + c : 4 * e + c + 1, :], (8, EZ)) for c in range(4)]

            @pl.loop(0, NT)
            def _(t):
                row = jnp.minimum(t * 8, NP - 8)
                scale = tables[pl.ds(2 * NP + row, 8), :]
                base = (
                    part[1] * tables[pl.ds(row, 8), :]
                    + part[2] * tables[pl.ds(NP + row, 8), :]
                    + part[3]
                )
                for k in range(ORDER):
                    put = pl.multiple_of(((e * NT + t) * ORDER + k) * 8, 8)
                    rt[pl.ds(put, 8), :] = (scale * float(_S[0, k] ** 2)) / (
                        base + part[0] * float(_LAM[k])
                    )

        @pl.loop(0, ORDER + 2)
        def _(x):
            for k in range(LX // 8):
                U[pl.ds(pl.multiple_of(x * LX + 8 * k, 8), 8), :] = zero_tile

        collect(0, everything)

        for c in range(4):

            def row_of(dx, dy, e):
                if (dx, dy) == (0, 0):
                    return cc[4 * e + c : 4 * e + c + 1, :]
                return cn[DIRS.index((-dx, -dy)), 4 * e + c : 4 * e + c + 1, :]

            for xs, dx in (((0,), -1), (range(1, ORDER - 1), 0), ((ORDER - 1,), 1)):
                first = row_of(dx, -1, 1)
                last = row_of(dx, 1, 0)
                low = jnp.broadcast_to(row_of(dx, 0, 0), (8, EZ))
                high = jnp.broadcast_to(row_of(dx, 0, 1), (8, EZ))
                for x in xs:
                    put = c * NQ + x * WY
                    cf[put : put + 1, :] = jnp.zeros((1, EZ), F32)
                    cf[put + 1 : put + 2, :] = first
                    cf[put + 2 : put + 10, :] = low
                    cf[put + 10 : put + 18, :] = high
                    cf[put + 18 : put + 19, :] = last
                    cf[put + 19 : put + 20, :] = jnp.zeros((1, EZ), F32)

        def load_z(ref, row):
            return [ref[pl.ds(row + z * WY, 8), :] for z in range(NODES)]

        def residual(x, y, coef):
            f = load_z(F, x * LX + y)
            here = (x + 1) * LX + y
            u = load_z(U, here)
            xa, xb = load_z(U, here - LX), load_z(U, here + LX)
            ya, yb = load_z(U, here - 1), load_z(U, here + 1)
            line = [from_below(u[-1])] + u + [from_above(u[0])]
            cx, cy, cz, m = coef
            diag = 2.0 * (cx + cy + cz) + m
            return [
                f[z]
                - (
                    diag * u[z]
                    - cx * (xa[z] + xb[z])
                    - cy * (ya[z] + yb[z])
                    - cz * (line[z] + line[z + 2])
                )
                for z in range(NODES)
            ]

        ROW_A, ROW_D, ROW_C = 1, 3, 11

        def z_forward(first, x, starts):
            for y in starts:
                if first:
                    g = load_z(F, x * LX + y)
                else:
                    g = residual(x, y, [cf[pl.ds(c * NQ + x * WY + y, 8), :] for c in range(4)])
                v = forward([from_below(g[-1])] + g + [from_above(g[0])])
                for k in range(ORDER):
                    zs[pl.ds(k * NQ + x * WY + y, 8), :] = v[k]

        def z_backward(starts):
            @pl.loop(0, ORDER)
            def _(x):
                for y in starts:
                    v = backward([zi[pl.ds(k * NQ + x * WY + y, 8), :] for k in range(ORDER)])
                    body = v[1:-1]
                    body[0] = body[0] + from_below(v[-1])
                    body[-1] = body[-1] + from_above(v[0])
                    for z in range(NODES):
                        PA[pl.ds(x * LX + z * WY + y, 8), :] = body[z]

            for x, ok in ((0, i > 0), (ORDER - 1, i < n_sx - 1)):

                @pl.when(jnp.logical_not(ok))
                def _():
                    for y in starts:
                        for z in range(NODES):
                            PA[pl.ds(x * LX + z * WY + y, 8), :] = zero_tile

            for y, start, ok in ((1, ROW_A, j > 0), (WY - 2, ROW_C, j < n_sy - 1)):
                if start in starts:

                    @pl.when(jnp.logical_not(ok))
                    def _():
                        for x in range(ORDER):
                            PA[pl.ds(x * LX + y, 8, stride=WY), :] = zero_tile

        def element(e, second):
            @pl.loop(0, NT)
            def _(t):
                p = jnp.minimum(t * 8, NP - 8)
                v = forward(
                    [zs[pl.ds(p * WY + 1 + 8 * e + y, 8, stride=WY), :] for y in range(ORDER)]
                )
                for k in range(ORDER):
                    ys[pl.ds(k * NP + p, 8), :] = v[k]

            @pl.loop(0, NT)
            def _(t):
                row = jnp.minimum(t * 8, NP - 8) * ORDER
                v = forward([ys[pl.ds(row + x, 8, stride=ORDER), :] for x in range(ORDER)])
                table = (e * NT + t) * ORDER * 8
                v = [
                    v[k] * rt[pl.ds(pl.multiple_of(table + 8 * k, 8), 8), :] for k in range(ORDER)
                ]
                v = backward(v)
                for x in range(ORDER):
                    yt[pl.ds(row + x, 8, stride=ORDER), :] = v[x]

            @pl.loop(0, NT)
            def _(t):
                p = jnp.minimum(t * 8, NP - 8)
                v = backward([yt[pl.ds(k * NP + p, 8), :] for k in range(ORDER)])
                shared = (0, 1) if e else (8, 9)
                for y in range(ORDER):
                    if y in shared:
                        spare = pl.ds((y - shared[0]) * NP + p, 8)
                        if not second:
                            ov[spare, :] = v[y]
                            continue
                        v[y] = v[y] + ov[spare, :]
                    zi[pl.ds(p * WY + 1 + 8 * e + y, 8, stride=WY), :] = v[y]

        @pl.loop(0, ORDER)
        def _(x):
            z_forward(True, x, (ROW_A, ROW_D, ROW_C))

        element(1, False)
        z_backward((ROW_C,))
        post(1, PA, lambda dx, dy, g: g == 1)
        element(0, True)
        z_backward((ROW_A, ROW_D))
        post(1, PA, lambda dx, dy, g: g == 0)

        @pl.loop(0, ORDER)
        def _(x):
            for k in range(LX // 8):
                row = pl.multiple_of(x * LX + 8 * k, 8)
                U[pl.ds(row + LX, 8), :] = PA[pl.ds(row, 8), :]

        collect(1, lambda dx, dy, g: g == 1)

        @pl.loop(3, 7)
        def _(x):
            z_forward(False, x, (ROW_A, ROW_D))

        collect(1, lambda dx, dy, g: g == 0 and dy == 0)

        @pl.loop(0, 6)
        def _(t):
            z_forward(False, jnp.where(t < 3, t, t + 4), (ROW_A, ROW_D))

        element(0, False)
        z_backward((ROW_A,))
        post(2, PA, lambda dx, dy, g: g == 0)
        collect(1, lambda dx, dy, g: g == 0 and dy != 0)

        @pl.loop(0, ORDER)
        def _(x):
            z_forward(False, x, (ROW_C,))

        element(1, True)
        z_backward((ROW_D, ROW_C))
        post(2, PA, lambda dx, dy, g: g == 1)

        @pl.loop(0, ORDER)
        def _(x):
            for k in range(LX // 8):
                row = pl.multiple_of(x * LX + 8 * k, 8)
                U[pl.ds(row + LX, 8), :] = U[pl.ds(row + LX, 8), :] + PA[pl.ds(row, 8), :]

        collect(2, lambda dx, dy, g: g == 0)
        collect(2, lambda dx, dy, g: g == 1)

        weights = [((NODES - 1 - t) / (NODES - 1), t / (NODES - 1)) for t in range(NODES)]
        coefs = [
            [jnp.broadcast_to(cc[4 * h + c : 4 * h + c + 1, :], (8, EZ)) for c in range(4)]
            for h in range(EY)
        ]

        def last(x, carry):
            wx = x.astype(F32) * (1.0 / (NODES - 1))
            carry = list(carry)
            for h in range(EY):
                r = residual(x + 1, 2 + 8 * h, coefs[h])
                for z in range(NODES):
                    ro[pl.ds(x * LX + z * WY + 8 * h, 8), :] = r[z]
                for c in range(2):
                    total = None
                    for z in range(NODES):
                        if weights[z][c] == 0.0:
                            continue
                        term = weights[z][c] * r[z]
                        total = term if total is None else total + term
                    carry[4 * h + c] = carry[4 * h + c] + (1.0 - wx) * total
                    carry[4 * h + 2 + c] = carry[4 * h + 2 + c] + wx * total
            return tuple(carry)

        acc = lax.fori_loop(0, NODES, last, tuple([zero_tile] * 8))
        wy1 = sub.astype(F32) * (1.0 / (NODES - 1))
        for h in range(EY):
            for a in range(2):
                for b in range(2):
                    for c in range(2):
                        w = wy1 if b else 1.0 - wy1
                        row = jnp.sum(acc[4 * h + 2 * a + c] * w, axis=0, keepdims=True)
                        v = 4 * a + 2 * b + c
                        mo[v : v + 1, EZ * h : EZ * (h + 1)] = row
        moments = exact_dot(mo[...], perm[...], 0)
        groups = GRP_DEV * n_sy
        column = group[...] - i * groups
        onehot = jnp.where(
            lax.broadcasted_iota(jnp.int32, (groups, EY * EZ), 0) == column, 1.0, 0.0
        ).astype(BF16)
        partial = exact_dot(moments, onehot, 1)
        per = EZ // GRP_DEV
        for d in range(n_sy):
            block = partial[:, (d // per) * EZ : (d // per + 1) * EZ]
            shift = (d % per) * GRP_DEV
            sb[d] = block if shift == 0 else pltpu.roll(block, EZ - shift, 1)

        def copy4(d):
            dest = lax.rem(j + d, n_sy)
            return pltpu.make_async_remote_copy(
                src_ref=sb.at[dest],
                dst_ref=rb.at[d - 1],
                send_sem=s4.at[d - 1],
                recv_sem=r4.at[d - 1],
                device_id=(i, dest),
                device_id_type=MESH,
            )

        for d in range(1, n_sy):
            copy4(d).start()

        def slots(ref, base):
            halves = [
                jnp.concatenate(
                    [ref[pl.ds(base + 8 * h + y, 8, stride=WY), :] for y in range(8)], axis=0
                )
                for h in range(EY)
            ]
            return exact_dot(jnp.concatenate(halves, axis=1), perm[...], 0)

        @pl.loop(0, NODES)
        def _(x):
            rows = pl.ds(pl.multiple_of(x * 64, 64), 64)
            sm_out[rows, :] = slots(U, (x + 2) * LX + 2)
            fr_out[rows, :] = slots(ro, x * LX)

        for r in range(len(ROUNDS)):
            for n, (dx, dy, g, tiles) in enumerate(ROUNDS[r]):

                @pl.when(exists(dx, dy))
                def _():
                    copy_of(r, n).wait_send()

        total = sb[j]
        for d in range(1, n_sy):
            copy4(d).wait()
            total = total + rb[d - 1]
        co_out[...] = total[:, 0:GRP_DEV]

    return kernel


def solution(mesh):
    n_sx, n_sy = mesh.shape["sx"], mesh.shape["sy"]
    s0 = _S[0] ** 2
    column = np.concatenate(
        [np.repeat(_LAM, ORDER), np.tile(_LAM, ORDER), RELAX * np.outer(s0, s0).ravel()]
    ).astype(np.float32)

    def on_device(right_side, stretch, mass_term, slot_position, coarse_group):
        elements = right_side.shape[3]
        tables = jnp.broadcast_to(jnp.asarray(column)[:, None], (column.size, EZ))
        vmem = pl.BlockSpec(memory_space=pltpu.VMEM)
        V = lambda *shape: pltpu.VMEM(shape, F32)
        dma = lambda n: pltpu.SemaphoreType.DMA((n,))
        points = NODES**3
        scratch = [
            pltpu.VMEM((elements, elements), BF16),
            V(8, elements),
            V(8, EZ),
            V(ND, 8, EZ),
            V(4 * NQ, EZ),
            V(EY * NT * ORDER * 8, EZ),
            V(ORDER * LX, EZ),
            V((ORDER + 2) * LX, EZ),
            V(ORDER * LX, EZ),
            V(ORDER * NQ, EZ),
            V(ORDER * NQ, EZ),
            V(ORDER * NP, EZ),
            V(ORDER * NP, EZ),
            V(2 * NP, EZ),
            V(NODES * LX, EZ),
            V(8, elements),
            V(n_sy, 8, EZ),
            V(max(n_sy - 1, 1), 8, EZ),
        ]
        for messages in ROUNDS:
            for side in range(2):
                scratch += [V(8 * message_size(m), EZ) for m in messages]
            scratch += [dma(len(messages))] * 2
        scratch += [dma(max(n_sy - 1, 1))] * 2
        smoothed, fine, coarse = pl.pallas_call(
            make_kernel(n_sx, n_sy),
            out_shape=(
                jax.ShapeDtypeStruct((points, elements), F32),
                jax.ShapeDtypeStruct((points, elements), F32),
                jax.ShapeDtypeStruct((8, GRP_DEV), F32),
            ),
            in_specs=[vmem] * 6,
            out_specs=(vmem, vmem, vmem),
            scratch_shapes=scratch,
            compiler_params=pltpu.CompilerParams(
                collective_id=0, has_side_effects=True, vmem_limit_bytes=48 * 1024 * 1024
            ),
        )(
            right_side.reshape(points, elements),
            stretch,
            mass_term.reshape(1, elements),
            slot_position.reshape(1, elements),
            coarse_group.reshape(1, elements),
            tables,
        )
        shape = right_side.shape
        return smoothed.reshape(shape), fine.reshape(shape), coarse

    split = ("sx", "sy")
    field = P(None, None, None, split)
    return jax.shard_map(
        on_device,
        mesh=mesh,
        in_specs=(field, P(None, split), P(split), P(split), P(split)),
        out_specs=(field, field, P(None, split)),
        check_vma=False,
    )
```

```python
import numpy as np
import jax
import jax.numpy as jnp
from jax import lax
from jax.experimental import pallas as pl
from jax.experimental.pallas import tpu as pltpu
from jax.sharding import PartitionSpec as P

NODES = 8
EY = 2
EZ = 128
GRP_DEV = 16
RELAX = 0.35
ORDER = NODES + 2
F32 = jnp.float32
BF16 = jnp.bfloat16
MESH = pl.DeviceIdType.MESH

WY = EY * NODES + 4
LX = NODES * WY
NQ = ORDER * WY
NP = ORDER * ORDER
NT = 13
TY = EY * NODES

_m = np.arange(1, ORDER + 1, dtype=np.float64)
_S = np.sqrt(2.0 / (ORDER + 1)) * np.sin(np.pi * np.outer(_m, _m) / (ORDER + 1))
_LAM = 2.0 - 2.0 * np.cos(np.pi * _m / (ORDER + 1))
_C = _S / _S[0:1, :]
_HALF = ORDER // 2

DIRS = [(dx, dy) for dx in (-1, 0, 1) for dy in (-1, 0, 1) if (dx, dy) != (0, 0)]
ND = len(DIRS)


def forward(g):
    a = [g[i] + g[ORDER - 1 - i] for i in range(_HALF)]
    b = [g[i] - g[ORDER - 1 - i] for i in range(_HALF)]
    out = []
    for k in range(ORDER):
        part = a if k % 2 == 0 else b
        total = part[0]
        for i in range(1, _HALF):
            total = total + float(_C[i, k]) * part[i]
        out.append(total)
    return out


def backward(v):
    low, high = [], []
    for i in range(_HALF):
        sums = []
        for parity in (0, 1):
            total = None
            for k in range(parity, ORDER, 2):
                term = v[k] if i == 0 else float(_C[i, k]) * v[k]
                total = term if total is None else total + term
            sums.append(total)
        low.append(sums[0] + sums[1])
        high.append(sums[0] - sums[1])
    return low + high[::-1]


def split3(x):
    hi = x.astype(BF16)
    rest = x - hi.astype(F32)
    mid = rest.astype(BF16)
    low = (rest - mid.astype(F32)).astype(BF16)
    return hi, mid, low


def exact_dot(x, table, contract):
    dims = (((1,), (contract,)), ((), ()))
    parts = [lax.dot_general(s, table, dims, preferred_element_type=F32) for s in split3(x)]
    return parts[0] + (parts[1] + parts[2])


def edge_range(d, size, layers):
    if d > 0:
        return range(size - layers + 1, size + 1)
    return range(-1, layers - 1)


def slab_messages(layers, early):
    out = []
    for group, dy in ((early, 1 if early else -1), (1 - early, -1 if early else 1)):
        for dx in (0, -1, 1):
            xs = range(-1, NODES + 1) if dx == 0 else edge_range(dx, NODES, layers)
            ys = edge_range(dy, TY, layers)
            far_x = None if dx == 0 else (xs[0] if dx > 0 else xs[-1])
            far_y = ys[0] if dy > 0 else ys[-1]
            tiles = [("v", x, y) for y in ys for x in xs if (x, y) != (far_x, far_y)]
            out.append((dx, dy, group, tiles))
        for dx in (-1, 1):
            xs = edge_range(dx, NODES, layers)
            start = 9 if group else -1
            tiles = [("h", x, z, start) for x in xs for z in range(NODES)]
            if group != early:
                tiles += [("v", x, y) for x in xs for y in (7, 8)]
            out.append((dx, 0, group, tiles))
    return out


def field_messages():
    out = []
    for dx, dy in DIRS:
        xs = range(NODES) if dx == 0 else ((NODES - 1,) if dx > 0 else (0,))
        if dy == 0:
            tiles = [("h", x, z, y) for x in xs for z in range(NODES) for y in (0, 8)]
        else:
            tiles = [("v", x, TY - 1 if dy > 0 else 0) for x in xs]
        out.append((dx, dy, 0, tiles))
    return out


ROUNDS = (field_messages(), slab_messages(3, 1), slab_messages(2, 0))


def message_size(message):
    return len(message[3]) + (1 if message in ROUNDS[0] else 0)


def tile_at(tile, shift_x, shift_y):
    if tile[0] == "v":
        return pl.ds((tile[1] + shift_x) * LX + tile[2] + shift_y, 8, stride=WY)
    return pl.ds(((tile[1] + shift_x) * NODES + tile[2]) * WY + tile[3] + shift_y, 8)


def make_kernel(n_sx, n_sy):
    def kernel(*refs):
        (rs_in, stretch_in, mass_in, slot_in, group_in, sm_out, fr_out, co_out) = refs[:8]
        (perm, cb, cc, cn, cf, rt, F, U, PA, zs, zi, ys, yt, ov, ro, mo, sb, rb) = refs[8:26]
        (rs, stretch, mass, slot, group, tables, isem) = refs[26:33]
        at = 33
        rounds = []
        for messages in ROUNDS:
            n = len(messages)
            rounds.append(
                (messages, refs[at : at + n], refs[at + n : at + 2 * n]) + refs[at + 2 * n : at + 2 * n + 2]
            )
            at += 2 * n + 2
        s4, r4 = refs[at : at + 2]
        loads = [
            pltpu.make_async_copy(src, dst, isem.at[n])
            for n, (src, dst) in enumerate(
                (
                    (slot_in, slot),
                    (stretch_in, stretch),
                    (mass_in, mass),
                    (rs_in, rs),
                    (group_in, group),
                )
            )
        ]
        for load in loads:
            load.start()
        i = lax.axis_index("sx")
        j = lax.axis_index("sy")

        def exists(dx, dy):
            ok = None
            for pos, d, size in ((i, dx, n_sx), (j, dy, n_sy)):
                cond = pos < size - 1 if d > 0 else (pos > 0 if d < 0 else None)
                if cond is not None:
                    ok = cond if ok is None else jnp.logical_and(ok, cond)
            return ok

        barrier = pltpu.get_barrier_semaphore()
        count = n_sy - 1
        for d in range(1, n_sy):
            pl.semaphore_signal(
                barrier, inc=1, device_id=(i, lax.rem(j + d, n_sy)), device_id_type=MESH
            )
        for dx, dy in DIRS:
            if dx == 0:
                continue
            ok = exists(dx, dy)
            count = count + ok.astype(jnp.int32)

            @pl.when(ok)
            def _():
                pl.semaphore_signal(
                    barrier, inc=1, device_id=(i + dx, j + dy), device_id_type=MESH
                )

        lane = lax.broadcasted_iota(jnp.int32, (8, EZ), 1)
        sub = lax.broadcasted_iota(jnp.int32, (8, EZ), 0)
        zero_tile = jnp.zeros((8, EZ), F32)

        def from_below(v):
            return jnp.where(lane == 0, 0.0, pltpu.roll(v, 1, 1))

        def from_above(v):
            return jnp.where(lane == EZ - 1, 0.0, pltpu.roll(v, EZ - 1, 1))

        for n in range(ND):
            cn[n] = zero_tile

        for x in range(ORDER):
            for y in (range(WY) if x in (0, ORDER - 1) else (0, 1, WY - 2, WY - 1)):
                F[pl.ds(x * LX + y, 8, stride=WY), :] = zero_tile
            for y in (0, WY - 1):
                PA[pl.ds(x * LX + y, 8, stride=WY), :] = zero_tile

        @pl.loop(0, ORDER + 2)
        def _(x):
            for k in range(LX // 8):
                U[pl.ds(pl.multiple_of(x * LX + 8 * k, 8), 8), :] = zero_tile

        s0 = _S[0] ** 2
        for l in range(ORDER):
            for k in range(ORDER):
                c = l * ORDER + k
                values = (_LAM[l], _LAM[k], RELAX * s0[l] * s0[k])
                for part, value in enumerate(values):
                    at_row = part * NP + c
                    tables[at_row : at_row + 1, :] = jnp.full((1, EZ), float(value), F32)

        for load in loads:
            load.wait()
        positions = lax.broadcasted_iota(jnp.int32, (EY * EZ, EY * EZ), 0)
        perm[...] = jnp.where(positions == slot[...], 1.0, 0.0).astype(BF16)
        cb[...] = jnp.zeros_like(cb)
        cb[0:3, :] = stretch[...]
        cb[3:4, :] = mass[...]
        ordered = exact_dot(cb[...], perm[...], 1)
        cc[0:4, :] = ordered[0:4, 0:EZ]
        cc[4:8, :] = ordered[0:4, EZ : 2 * EZ]
        for x in range(NODES):
            got = exact_dot(rs[x * 64 : x * 64 + 64, :], perm[...], 1)
            for y in range(TY):
                part = got[8 * (y % 8) : 8 * (y % 8) + 8, EZ * (y // 8) : EZ * (y // 8 + 1)]
                F[tile_at(("v", x, y), 1, 2), :] = part

        pl.semaphore_wait(barrier, count)

        def copy_of(r, n):
            messages, send, recv, ssem, rsem = rounds[r]
            dx, dy = messages[n][:2]
            return pltpu.make_async_remote_copy(
                src_ref=send[n],
                dst_ref=recv[n],
                send_sem=ssem.at[n],
                recv_sem=rsem.at[n],
                device_id=(i + dx, j + dy),
                device_id_type=MESH,
            )

        def post(r, source, wanted):
            messages, send = rounds[r][:2]
            for n, (dx, dy, g, tiles) in enumerate(messages):
                if not wanted(dx, dy, g):
                    continue

                @pl.when(exists(dx, dy))
                def _():
                    for k, tile in enumerate(tiles):
                        send[n][8 * k : 8 * k + 8, :] = source[tile_at(tile, 1, 2), :]
                    if r == 0:
                        send[n][8 * len(tiles) : 8 * len(tiles) + 8, :] = cc[...]
                    copy_of(r, n).start()

        def collect(r, wanted):
            messages, send, recv = rounds[r][:3]
            for n, (dx, dy, g, tiles) in enumerate(messages):
                if not wanted(dx, dy, g):
                    continue

                @pl.when(exists(-dx, -dy))
                def _():
                    copy_of(r, n).wait_recv()
                    for k, tile in enumerate(tiles):
                        got = recv[n][8 * k : 8 * k + 8, :]
                        if r == 0:
                            F[tile_at(tile, 1 - NODES * dx, 2 - TY * dy), :] = got
                        else:
                            here = tile_at(tile, 2 - NODES * dx, 2 - TY * dy)
                            U[here, :] = U[here, :] + got
                    if r == 0:
                        cn[n] = recv[n][8 * len(tiles) : 8 * len(tiles) + 8, :]

        def load_z(ref, row):
            return [ref[pl.ds(row + z * WY, 8), :] for z in range(NODES)]

        def residual(x, y, coef):
            f = load_z(F, x * LX + y)
            here = (x + 1) * LX + y
            u = load_z(U, here)
            xa, xb = load_z(U, here - LX), load_z(U, here + LX)
            ya, yb = load_z(U, here - 1), load_z(U, here + 1)
            line = [from_below(u[-1])] + u + [from_above(u[0])]
            cx, cy, cz, m = coef
            diag = 2.0 * (cx + cy + cz) + m
            return [
                f[z]
                - (
                    diag * u[z]
                    - cx * (xa[z] + xb[z])
                    - cy * (ya[z] + yb[z])
                    - cz * (line[z] + line[z + 2])
                )
                for z in range(NODES)
            ]

        ROW_A, ROW_D, ROW_C = 1, 3, 11

        def z_forward(first, x, starts):
            for y in starts:
                if first:
                    g = load_z(F, x * LX + y)
                else:
                    g = residual(x, y, [cf[pl.ds(c * NQ + x * WY + y, 8), :] for c in range(4)])
                v = forward([from_below(g[-1])] + g + [from_above(g[0])])
                for k in range(ORDER):
                    zs[pl.ds(k * NQ + x * WY + y, 8), :] = v[k]

        everything = lambda dx, dy, g: True
        post(0, F, everything)

        for e in range(EY):
            part = [jnp.broadcast_to(cc[4 * e + c : 4 * e + c + 1, :], (8, EZ)) for c in range(4)]

            @pl.loop(0, NT)
            def _(t):
                row = jnp.minimum(t * 8, NP - 8)
                scale = tables[pl.ds(2 * NP + row, 8), :]
                base = (
                    part[1] * tables[pl.ds(row, 8), :]
                    + part[2] * tables[pl.ds(NP + row, 8), :]
                    + part[3]
                )
                for k in range(ORDER):
                    put = pl.multiple_of(((e * NT + t) * ORDER + k) * 8, 8)
                    rt[pl.ds(put, 8), :] = (scale * float(_S[0, k] ** 2)) / (
                        base + part[0] * float(_LAM[k])
                    )

        @pl.loop(1, ORDER - 1)
        def _(x):
            z_forward(True, x, (2, 10))

        collect(0, everything)

        for c in range(4):

            def row_of(dx, dy, e):
                if (dx, dy) == (0, 0):
                    return cc[4 * e + c : 4 * e + c + 1, :]
                return cn[DIRS.index((-dx, -dy)), 4 * e + c : 4 * e + c + 1, :]

            for xs, dx in (((0,), -1), (range(1, ORDER - 1), 0), ((ORDER - 1,), 1)):
                first = row_of(dx, -1, 1)
                last = row_of(dx, 1, 0)
                low = jnp.broadcast_to(row_of(dx, 0, 0), (8, EZ))
                high = jnp.broadcast_to(row_of(dx, 0, 1), (8, EZ))
                for x in xs:
                    put = c * NQ + x * WY
                    cf[put : put + 1, :] = jnp.zeros((1, EZ), F32)
                    cf[put + 1 : put + 2, :] = first
                    cf[put + 2 : put + 10, :] = low
                    cf[put + 10 : put + 18, :] = high
                    cf[put + 18 : put + 19, :] = last
                    cf[put + 19 : put + 20, :] = jnp.zeros((1, EZ), F32)

        def z_backward(starts):
            @pl.loop(0, ORDER)
            def _(x):
                for y in starts:
                    v = backward([zi[pl.ds(k * NQ + x * WY + y, 8), :] for k in range(ORDER)])
                    body = v[1:-1]
                    body[0] = body[0] + from_below(v[-1])
                    body[-1] = body[-1] + from_above(v[0])
                    for z in range(NODES):
                        PA[pl.ds(x * LX + z * WY + y, 8), :] = body[z]

            for x, ok in ((0, i > 0), (ORDER - 1, i < n_sx - 1)):

                @pl.when(jnp.logical_not(ok))
                def _():
                    for y in starts:
                        for z in range(NODES):
                            PA[pl.ds(x * LX + z * WY + y, 8), :] = zero_tile

            for y, start, ok in ((1, ROW_A, j > 0), (WY - 2, ROW_C, j < n_sy - 1)):
                if start in starts:

                    @pl.when(jnp.logical_not(ok))
                    def _():
                        for x in range(ORDER):
                            PA[pl.ds(x * LX + y, 8, stride=WY), :] = zero_tile

        def element(e, second):
            @pl.loop(0, NT)
            def _(t):
                p = jnp.minimum(t * 8, NP - 8)
                v = forward(
                    [zs[pl.ds(p * WY + 1 + 8 * e + y, 8, stride=WY), :] for y in range(ORDER)]
                )
                for k in range(ORDER):
                    ys[pl.ds(k * NP + p, 8), :] = v[k]

            @pl.loop(0, NT)
            def _(t):
                row = jnp.minimum(t * 8, NP - 8) * ORDER
                v = forward([ys[pl.ds(row + x, 8, stride=ORDER), :] for x in range(ORDER)])
                table = (e * NT + t) * ORDER * 8
                v = [
                    v[k] * rt[pl.ds(pl.multiple_of(table + 8 * k, 8), 8), :] for k in range(ORDER)
                ]
                v = backward(v)
                for x in range(ORDER):
                    yt[pl.ds(row + x, 8, stride=ORDER), :] = v[x]

            @pl.loop(0, NT)
            def _(t):
                p = jnp.minimum(t * 8, NP - 8)
                v = backward([yt[pl.ds(k * NP + p, 8), :] for k in range(ORDER)])
                shared = (0, 1) if e else (8, 9)
                for y in range(ORDER):
                    if y in shared:
                        spare = pl.ds((y - shared[0]) * NP + p, 8)
                        if not second:
                            ov[spare, :] = v[y]
                            continue
                        v[y] = v[y] + ov[spare, :]
                    zi[pl.ds(p * WY + 1 + 8 * e + y, 8, stride=WY), :] = v[y]

        for x in (0, ORDER - 1):
            z_forward(True, x, (ROW_A, ROW_D, ROW_C))
        for y in (1, WY - 2):
            g = [F[pl.ds(LX + z * WY + y, 8, stride=LX), :] for z in range(NODES)]
            v = forward([from_below(g[-1])] + g + [from_above(g[0])])
            for k in range(ORDER):
                zs[pl.ds(k * NQ + WY + y, 8, stride=WY), :] = v[k]

        element(1, False)
        z_backward((ROW_C,))
        post(1, PA, lambda dx, dy, g: g == 1)
        element(0, True)
        z_backward((ROW_A, ROW_D))
        post(1, PA, lambda dx, dy, g: g == 0)

        @pl.loop(0, ORDER)
        def _(x):
            for k in range(LX // 8):
                row = pl.multiple_of(x * LX + 8 * k, 8)
                U[pl.ds(row + LX, 8), :] = PA[pl.ds(row, 8), :]

        collect(1, lambda dx, dy, g: g == 1)

        @pl.loop(3, 7)
        def _(x):
            z_forward(False, x, (ROW_A, ROW_D))

        collect(1, lambda dx, dy, g: g == 0 and dy == 0)

        @pl.loop(0, 6)
        def _(t):
            z_forward(False, jnp.where(t < 3, t, t + 4), (ROW_A, ROW_D))

        element(0, False)
        z_backward((ROW_A,))
        post(2, PA, lambda dx, dy, g: g == 0)
        collect(1, lambda dx, dy, g: g == 0 and dy != 0)

        @pl.loop(0, ORDER)
        def _(x):
            z_forward(False, x, (ROW_C,))

        element(1, True)
        z_backward((ROW_D, ROW_C))
        post(2, PA, lambda dx, dy, g: g == 1)

        @pl.loop(0, ORDER)
        def _(x):
            for k in range(LX // 8):
                row = pl.multiple_of(x * LX + 8 * k, 8)
                U[pl.ds(row + LX, 8), :] = U[pl.ds(row + LX, 8), :] + PA[pl.ds(row, 8), :]

        collect(2, lambda dx, dy, g: g == 0)
        collect(2, lambda dx, dy, g: g == 1)

        weights = [((NODES - 1 - t) / (NODES - 1), t / (NODES - 1)) for t in range(NODES)]
        coefs = [
            [jnp.broadcast_to(cc[4 * h + c : 4 * h + c + 1, :], (8, EZ)) for c in range(4)]
            for h in range(EY)
        ]

        def last(x, carry):
            wx = x.astype(F32) * (1.0 / (NODES - 1))
            carry = list(carry)
            for h in range(EY):
                r = residual(x + 1, 2 + 8 * h, coefs[h])
                for z in range(NODES):
                    ro[pl.ds(x * LX + z * WY + 8 * h, 8), :] = r[z]
                for c in range(2):
                    total = None
                    for z in range(NODES):
                        if weights[z][c] == 0.0:
                            continue
                        term = weights[z][c] * r[z]
                        total = term if total is None else total + term
                    carry[4 * h + c] = carry[4 * h + c] + (1.0 - wx) * total
                    carry[4 * h + 2 + c] = carry[4 * h + 2 + c] + wx * total
            return tuple(carry)

        acc = lax.fori_loop(0, NODES, last, tuple([zero_tile] * 8))
        wy1 = sub.astype(F32) * (1.0 / (NODES - 1))
        for h in range(EY):
            for a in range(2):
                for b in range(2):
                    for c in range(2):
                        w = wy1 if b else 1.0 - wy1
                        row = jnp.sum(acc[4 * h + 2 * a + c] * w, axis=0, keepdims=True)
                        v = 4 * a + 2 * b + c
                        mo[v : v + 1, EZ * h : EZ * (h + 1)] = row
        moments = exact_dot(mo[...], perm[...], 0)
        groups = GRP_DEV * n_sy
        column = group[...] - i * groups
        onehot = jnp.where(
            lax.broadcasted_iota(jnp.int32, (groups, EY * EZ), 0) == column, 1.0, 0.0
        ).astype(BF16)
        partial = exact_dot(moments, onehot, 1)
        per = EZ // GRP_DEV
        for d in range(n_sy):
            block = partial[:, (d // per) * EZ : (d // per + 1) * EZ]
            shift = (d % per) * GRP_DEV
            sb[d] = block if shift == 0 else pltpu.roll(block, EZ - shift, 1)

        def copy4(d):
            dest = lax.rem(j + d, n_sy)
            return pltpu.make_async_remote_copy(
                src_ref=sb.at[dest],
                dst_ref=rb.at[d - 1],
                send_sem=s4.at[d - 1],
                recv_sem=r4.at[d - 1],
                device_id=(i, dest),
                device_id_type=MESH,
            )

        for d in range(1, n_sy):
            copy4(d).start()

        def slots(ref, base):
            halves = [
                jnp.concatenate(
                    [ref[pl.ds(base + 8 * h + y, 8, stride=WY), :] for y in range(8)], axis=0
                )
                for h in range(EY)
            ]
            return exact_dot(jnp.concatenate(halves, axis=1), perm[...], 0)

        @pl.loop(0, NODES)
        def _(x):
            rows = pl.ds(pl.multiple_of(x * 64, 64), 64)
            sm_out[rows, :] = slots(U, (x + 2) * LX + 2)
            fr_out[rows, :] = slots(ro, x * LX)

        for r in range(len(ROUNDS)):
            for n, (dx, dy, g, tiles) in enumerate(ROUNDS[r]):

                @pl.when(exists(dx, dy))
                def _():
                    copy_of(r, n).wait_send()

        total = sb[j]
        for d in range(1, n_sy):
            copy4(d).wait()
            total = total + rb[d - 1]
        co_out[...] = total[:, 0:GRP_DEV]

    return kernel


def solution(mesh):
    n_sx, n_sy = mesh.shape["sx"], mesh.shape["sy"]
    def on_device(right_side, stretch, mass_term, slot_position, coarse_group):
        elements = right_side.shape[3]
        vmem = pl.BlockSpec(memory_space=pltpu.VMEM)
        V = lambda *shape: pltpu.VMEM(shape, F32)
        dma = lambda n: pltpu.SemaphoreType.DMA((n,))
        points = NODES**3
        scratch = [
            pltpu.VMEM((elements, elements), BF16),
            V(8, elements),
            V(8, EZ),
            V(ND, 8, EZ),
            V(4 * NQ, EZ),
            V(EY * NT * ORDER * 8, EZ),
            V(ORDER * LX, EZ),
            V((ORDER + 2) * LX, EZ),
            V(ORDER * LX, EZ),
            V(ORDER * NQ, EZ),
            V(ORDER * NQ, EZ),
            V(ORDER * NP, EZ),
            V(ORDER * NP, EZ),
            V(2 * NP, EZ),
            V(NODES * LX, EZ),
            V(8, elements),
            V(n_sy, 8, EZ),
            V(max(n_sy - 1, 1), 8, EZ),
        ]
        scratch += [
            V(points, elements),
            V(3, elements),
            V(1, elements),
            pltpu.VMEM((1, elements), jnp.int32),
            pltpu.VMEM((1, elements), jnp.int32),
            V(3 * NP + 4, EZ),
            dma(5),
        ]
        for messages in ROUNDS:
            for side in range(2):
                scratch += [V(8 * message_size(m), EZ) for m in messages]
            scratch += [dma(len(messages))] * 2
        scratch += [dma(max(n_sy - 1, 1))] * 2
        smoothed, fine, coarse = pl.pallas_call(
            make_kernel(n_sx, n_sy),
            out_shape=(
                jax.ShapeDtypeStruct((points, elements), F32),
                jax.ShapeDtypeStruct((points, elements), F32),
                jax.ShapeDtypeStruct((8, GRP_DEV), F32),
            ),
            in_specs=[pl.BlockSpec(memory_space=pltpu.HBM)] * 5,
            out_specs=(vmem, vmem, vmem),
            scratch_shapes=scratch,
            compiler_params=pltpu.CompilerParams(
                collective_id=0, has_side_effects=True, vmem_limit_bytes=48 * 1024 * 1024
            ),
        )(
            *(
                pltpu.with_memory_space_constraint(array, pltpu.HBM)
                for array in (
                    right_side.reshape(points, elements),
                    stretch,
                    mass_term.reshape(1, elements),
                    slot_position.reshape(1, elements),
                    coarse_group.reshape(1, elements),
                )
            ),
        )
        shape = right_side.shape
        return smoothed.reshape(shape), fine.reshape(shape), coarse

    split = ("sx", "sy")
    field = P(None, None, None, split)
    return jax.shard_map(
        on_device,
        mesh=mesh,
        in_specs=(field, P(None, split), P(split), P(split), P(split)),
        out_specs=(field, field, P(None, split)),
        check_vma=False,
    )
```

```python
import numpy as np
import jax
import jax.numpy as jnp
from jax import lax
from jax.experimental import pallas as pl
from jax.experimental.pallas import tpu as pltpu
from jax.sharding import PartitionSpec as P

NODES = 8
EY = 2
EZ = 128
GRP_DEV = 16
RELAX = 0.35
ORDER = NODES + 2
F32 = jnp.float32
BF16 = jnp.bfloat16
MESH = pl.DeviceIdType.MESH

WY = EY * NODES + 4
LX = NODES * WY
NQ = ORDER * WY
NP = ORDER * ORDER
NT = 13
TY = EY * NODES

_m = np.arange(1, ORDER + 1, dtype=np.float64)
_S = np.sqrt(2.0 / (ORDER + 1)) * np.sin(np.pi * np.outer(_m, _m) / (ORDER + 1))
_LAM = 2.0 - 2.0 * np.cos(np.pi * _m / (ORDER + 1))
_C = _S / _S[0:1, :]
_HALF = ORDER // 2

DIRS = [(dx, dy) for dx in (-1, 0, 1) for dy in (-1, 0, 1) if (dx, dy) != (0, 0)]
ND = len(DIRS)


def forward(g):
    a = [g[i] + g[ORDER - 1 - i] for i in range(_HALF)]
    b = [g[i] - g[ORDER - 1 - i] for i in range(_HALF)]
    out = []
    for k in range(ORDER):
        part = a if k % 2 == 0 else b
        total = part[0]
        for i in range(1, _HALF):
            total = total + float(_C[i, k]) * part[i]
        out.append(total)
    return out


def backward(v):
    low, high = [], []
    for i in range(_HALF):
        sums = []
        for parity in (0, 1):
            total = None
            for k in range(parity, ORDER, 2):
                term = v[k] if i == 0 else float(_C[i, k]) * v[k]
                total = term if total is None else total + term
            sums.append(total)
        low.append(sums[0] + sums[1])
        high.append(sums[0] - sums[1])
    return low + high[::-1]


def split3(x):
    hi = x.astype(BF16)
    rest = x - hi.astype(F32)
    mid = rest.astype(BF16)
    low = (rest - mid.astype(F32)).astype(BF16)
    return hi, mid, low


def exact_dot(x, table, contract):
    dims = (((1,), (contract,)), ((), ()))
    parts = [lax.dot_general(s, table, dims, preferred_element_type=F32) for s in split3(x)]
    return parts[0] + (parts[1] + parts[2])


def edge_range(d, size, layers):
    if d > 0:
        return range(size - layers + 1, size + 1)
    return range(-1, layers - 1)


def slab_messages(layers, early):
    out = []
    for group, dy in ((early, 1 if early else -1), (1 - early, -1 if early else 1)):
        for dx in (0, -1, 1):
            xs = range(-1, NODES + 1) if dx == 0 else edge_range(dx, NODES, layers)
            ys = edge_range(dy, TY, layers)
            far_x = None if dx == 0 else (xs[0] if dx > 0 else xs[-1])
            far_y = ys[0] if dy > 0 else ys[-1]
            tiles = [("v", x, y) for y in ys for x in xs if (x, y) != (far_x, far_y)]
            out.append((dx, dy, group, tiles))
        for dx in (-1, 1):
            xs = edge_range(dx, NODES, layers)
            start = 9 if group else -1
            tiles = [("h", x, z, start) for x in xs for z in range(NODES)]
            if group != early:
                tiles += [("v", x, y) for x in xs for y in (7, 8)]
            out.append((dx, 0, group, tiles))
    return out


def field_messages():
    out = []
    for dx, dy in DIRS:
        xs = range(NODES) if dx == 0 else ((NODES - 1,) if dx > 0 else (0,))
        if dy == 0:
            tiles = [("h", x, z, y) for x in xs for z in range(NODES) for y in (0, 8)]
        else:
            tiles = [("v", x, TY - 1 if dy > 0 else 0) for x in xs]
        out.append((dx, dy, 0, tiles))
    return out


ROUNDS = (field_messages(), slab_messages(3, 1), slab_messages(2, 0))


def message_size(message):
    return len(message[3]) + (1 if message in ROUNDS[0] else 0)


def tile_at(tile, shift_x, shift_y):
    if tile[0] == "v":
        return pl.ds((tile[1] + shift_x) * LX + tile[2] + shift_y, 8, stride=WY)
    return pl.ds(((tile[1] + shift_x) * NODES + tile[2]) * WY + tile[3] + shift_y, 8)


def make_kernel(n_sx, n_sy):
    def kernel(*refs):
        (rs_in, stretch_in, mass_in, slot_in, group_in, sm_out, fr_out, co_out) = refs[:8]
        (perm, cb, cc, cn, cf, rt, F, U, PA, zs, zi, ys, yt, ov, ro, mo, sb, rb) = refs[8:26]
        (rs, stretch, mass, slot, group, tables, isem) = refs[26:33]
        at = 33
        rounds = []
        for messages in ROUNDS:
            n = len(messages)
            rounds.append(
                (messages, refs[at : at + n], refs[at + n : at + 2 * n]) + refs[at + 2 * n : at + 2 * n + 2]
            )
            at += 2 * n + 2
        s4, r4 = refs[at : at + 2]
        loads = [
            pltpu.make_async_copy(src, dst, isem.at[n])
            for n, (src, dst) in enumerate(
                (
                    (slot_in, slot),
                    (stretch_in, stretch),
                    (mass_in, mass),
                    (rs_in, rs),
                    (group_in, group),
                )
            )
        ]
        for load in loads:
            load.start()
        i = lax.axis_index("sx")
        j = lax.axis_index("sy")

        def exists(dx, dy):
            ok = None
            for pos, d, size in ((i, dx, n_sx), (j, dy, n_sy)):
                cond = pos < size - 1 if d > 0 else (pos > 0 if d < 0 else None)
                if cond is not None:
                    ok = cond if ok is None else jnp.logical_and(ok, cond)
            return ok

        barrier = pltpu.get_barrier_semaphore()
        count = n_sy - 1
        for d in range(1, n_sy):
            pl.semaphore_signal(
                barrier, inc=1, device_id=(i, lax.rem(j + d, n_sy)), device_id_type=MESH
            )
        for dx, dy in DIRS:
            if dx == 0:
                continue
            ok = exists(dx, dy)
            count = count + ok.astype(jnp.int32)

            @pl.when(ok)
            def _():
                pl.semaphore_signal(
                    barrier, inc=1, device_id=(i + dx, j + dy), device_id_type=MESH
                )

        lane = lax.broadcasted_iota(jnp.int32, (8, EZ), 1)
        sub = lax.broadcasted_iota(jnp.int32, (8, EZ), 0)
        zero_tile = jnp.zeros((8, EZ), F32)

        def from_below(v):
            return jnp.where(lane == 0, 0.0, pltpu.roll(v, 1, 1))

        def from_above(v):
            return jnp.where(lane == EZ - 1, 0.0, pltpu.roll(v, EZ - 1, 1))

        for n in range(ND):
            cn[n] = zero_tile

        for x in range(ORDER):
            for y in (range(WY) if x in (0, ORDER - 1) else (0, 1, WY - 2, WY - 1)):
                F[pl.ds(x * LX + y, 8, stride=WY), :] = zero_tile
            for y in (0, WY - 1):
                PA[pl.ds(x * LX + y, 8, stride=WY), :] = zero_tile

        @pl.loop(0, ORDER + 2)
        def _(x):
            for k in range(LX // 8):
                U[pl.ds(pl.multiple_of(x * LX + 8 * k, 8), 8), :] = zero_tile

        s0 = _S[0] ** 2
        for l in range(ORDER):
            for k in range(ORDER):
                c = l * ORDER + k
                values = (_LAM[l], _LAM[k], RELAX * s0[l] * s0[k])
                for part, value in enumerate(values):
                    at_row = part * NP + c
                    tables[at_row : at_row + 1, :] = jnp.full((1, EZ), float(value), F32)

        for load in loads:
            load.wait()
        positions = lax.broadcasted_iota(jnp.int32, (EY * EZ, EY * EZ), 0)
        perm[...] = jnp.where(positions == slot[...], 1.0, 0.0).astype(BF16)
        cb[...] = jnp.zeros_like(cb)
        cb[0:3, :] = stretch[...]
        cb[3:4, :] = mass[...]
        ordered = exact_dot(cb[...], perm[...], 1)
        cc[0:4, :] = ordered[0:4, 0:EZ]
        cc[4:8, :] = ordered[0:4, EZ : 2 * EZ]
        for x in range(NODES):
            got = exact_dot(rs[x * 64 : x * 64 + 64, :], perm[...], 1)
            for y in range(TY):
                part = got[8 * (y % 8) : 8 * (y % 8) + 8, EZ * (y // 8) : EZ * (y // 8 + 1)]
                F[tile_at(("v", x, y), 1, 2), :] = part

        pl.semaphore_wait(barrier, count)

        def copy_of(r, n):
            messages, send, recv, ssem, rsem = rounds[r]
            dx, dy = messages[n][:2]
            return pltpu.make_async_remote_copy(
                src_ref=send[n],
                dst_ref=recv[n],
                send_sem=ssem.at[n],
                recv_sem=rsem.at[n],
                device_id=(i + dx, j + dy),
                device_id_type=MESH,
            )

        def post(r, source, wanted):
            messages, send = rounds[r][:2]
            for n, (dx, dy, g, tiles) in enumerate(messages):
                if not wanted(dx, dy, g):
                    continue

                @pl.when(exists(dx, dy))
                def _():
                    for k, tile in enumerate(tiles):
                        send[n][8 * k : 8 * k + 8, :] = source[tile_at(tile, 1, 2), :]
                    if r == 0:
                        send[n][8 * len(tiles) : 8 * len(tiles) + 8, :] = cc[...]
                    copy_of(r, n).start()

        def collect(r, wanted):
            messages, send, recv = rounds[r][:3]
            for n, (dx, dy, g, tiles) in enumerate(messages):
                if not wanted(dx, dy, g):
                    continue

                @pl.when(exists(-dx, -dy))
                def _():
                    copy_of(r, n).wait_recv()
                    for k, tile in enumerate(tiles):
                        got = recv[n][8 * k : 8 * k + 8, :]
                        if r == 0:
                            F[tile_at(tile, 1 - NODES * dx, 2 - TY * dy), :] = got
                        else:
                            here = tile_at(tile, 2 - NODES * dx, 2 - TY * dy)
                            U[here, :] = U[here, :] + got
                    if r == 0:
                        cn[n] = recv[n][8 * len(tiles) : 8 * len(tiles) + 8, :]

        def load_z(ref, row):
            return [ref[pl.ds(row + z * WY, 8), :] for z in range(NODES)]

        def residual(x, y, coef):
            f = load_z(F, x * LX + y)
            here = (x + 1) * LX + y
            u = load_z(U, here)
            xa, xb = load_z(U, here - LX), load_z(U, here + LX)
            ya, yb = load_z(U, here - 1), load_z(U, here + 1)
            line = [from_below(u[-1])] + u + [from_above(u[0])]
            cx, cy, cz, m = coef
            diag = 2.0 * (cx + cy + cz) + m
            return [
                f[z]
                - (
                    diag * u[z]
                    - cx * (xa[z] + xb[z])
                    - cy * (ya[z] + yb[z])
                    - cz * (line[z] + line[z + 2])
                )
                for z in range(NODES)
            ]

        ROW_A, ROW_D, ROW_C = 1, 3, 11

        def z_forward(first, x, starts):
            for y in starts:
                if first:
                    g = load_z(F, x * LX + y)
                else:
                    g = residual(x, y, [cf[pl.ds(c * NQ + x * WY + y, 8), :] for c in range(4)])
                v = forward([from_below(g[-1])] + g + [from_above(g[0])])
                for k in range(ORDER):
                    zs[pl.ds(k * NQ + x * WY + y, 8), :] = v[k]

        everything = lambda dx, dy, g: True
        post(0, F, everything)

        for e in range(EY):
            part = [jnp.broadcast_to(cc[4 * e + c : 4 * e + c + 1, :], (8, EZ)) for c in range(4)]

            @pl.loop(0, NT)
            def _(t):
                row = jnp.minimum(t * 8, NP - 8)
                scale = tables[pl.ds(2 * NP + row, 8), :]
                base = (
                    part[1] * tables[pl.ds(row, 8), :]
                    + part[2] * tables[pl.ds(NP + row, 8), :]
                    + part[3]
                )
                for k in range(ORDER):
                    put = pl.multiple_of(((e * NT + t) * ORDER + k) * 8, 8)
                    rt[pl.ds(put, 8), :] = (scale * float(_S[0, k] ** 2)) / (
                        base + part[0] * float(_LAM[k])
                    )

        @pl.loop(1, ORDER - 1)
        def _(x):
            z_forward(True, x, (2, 10))

        collect(0, everything)

        for c in range(4):

            def row_of(dx, dy, e):
                if (dx, dy) == (0, 0):
                    return cc[4 * e + c : 4 * e + c + 1, :]
                return cn[DIRS.index((-dx, -dy)), 4 * e + c : 4 * e + c + 1, :]

            for xs, dx in (((0,), -1), (range(1, ORDER - 1), 0), ((ORDER - 1,), 1)):
                first = row_of(dx, -1, 1)
                last = row_of(dx, 1, 0)
                low = jnp.broadcast_to(row_of(dx, 0, 0), (8, EZ))
                high = jnp.broadcast_to(row_of(dx, 0, 1), (8, EZ))
                for x in xs:
                    put = c * NQ + x * WY
                    cf[put : put + 1, :] = jnp.zeros((1, EZ), F32)
                    cf[put + 1 : put + 2, :] = first
                    cf[put + 2 : put + 10, :] = low
                    cf[put + 10 : put + 18, :] = high
                    cf[put + 18 : put + 19, :] = last
                    cf[put + 19 : put + 20, :] = jnp.zeros((1, EZ), F32)

        def z_backward(starts):
            @pl.loop(0, ORDER)
            def _(x):
                for y in starts:
                    v = backward([zi[pl.ds(k * NQ + x * WY + y, 8), :] for k in range(ORDER)])
                    body = v[1:-1]
                    body[0] = body[0] + from_below(v[-1])
                    body[-1] = body[-1] + from_above(v[0])
                    for z in range(NODES):
                        PA[pl.ds(x * LX + z * WY + y, 8), :] = body[z]

            for x, ok in ((0, i > 0), (ORDER - 1, i < n_sx - 1)):

                @pl.when(jnp.logical_not(ok))
                def _():
                    for y in starts:
                        for z in range(NODES):
                            PA[pl.ds(x * LX + z * WY + y, 8), :] = zero_tile

            for y, start, ok in ((1, ROW_A, j > 0), (WY - 2, ROW_C, j < n_sy - 1)):
                if start in starts:

                    @pl.when(jnp.logical_not(ok))
                    def _():
                        for x in range(ORDER):
                            PA[pl.ds(x * LX + y, 8, stride=WY), :] = zero_tile

        def element(e, second):
            @pl.loop(0, NT)
            def _(t):
                p = jnp.minimum(t * 8, NP - 8)
                v = forward(
                    [zs[pl.ds(p * WY + 1 + 8 * e + y, 8, stride=WY), :] for y in range(ORDER)]
                )
                for k in range(ORDER):
                    ys[pl.ds(k * NP + p, 8), :] = v[k]

            @pl.loop(0, NT)
            def _(t):
                row = jnp.minimum(t * 8, NP - 8) * ORDER
                v = forward([ys[pl.ds(row + x, 8, stride=ORDER), :] for x in range(ORDER)])
                table = (e * NT + t) * ORDER * 8
                v = [
                    v[k] * rt[pl.ds(pl.multiple_of(table + 8 * k, 8), 8), :] for k in range(ORDER)
                ]
                v = backward(v)
                for x in range(ORDER):
                    yt[pl.ds(row + x, 8, stride=ORDER), :] = v[x]

            @pl.loop(0, NT)
            def _(t):
                p = jnp.minimum(t * 8, NP - 8)
                v = backward([yt[pl.ds(k * NP + p, 8), :] for k in range(ORDER)])
                shared = (0, 1) if e else (8, 9)
                for y in range(ORDER):
                    if y in shared:
                        spare = pl.ds((y - shared[0]) * NP + p, 8)
                        if not second:
                            ov[spare, :] = v[y]
                            continue
                        v[y] = v[y] + ov[spare, :]
                    zi[pl.ds(p * WY + 1 + 8 * e + y, 8, stride=WY), :] = v[y]

        for x in (0, ORDER - 1):
            z_forward(True, x, (ROW_A, ROW_D, ROW_C))
        for y in (1, WY - 2):
            g = [F[pl.ds(LX + z * WY + y, 8, stride=LX), :] for z in range(NODES)]
            v = forward([from_below(g[-1])] + g + [from_above(g[0])])
            for k in range(ORDER):
                zs[pl.ds(k * NQ + WY + y, 8, stride=WY), :] = v[k]

        element(1, False)
        z_backward((ROW_C,))
        post(1, PA, lambda dx, dy, g: g == 1)
        element(0, True)
        z_backward((ROW_A, ROW_D))
        post(1, PA, lambda dx, dy, g: g == 0)

        @pl.loop(0, ORDER)
        def _(x):
            for k in range(LX // 8):
                row = pl.multiple_of(x * LX + 8 * k, 8)
                U[pl.ds(row + LX, 8), :] = PA[pl.ds(row, 8), :]

        @pl.loop(3, 7)
        def _(x):
            z_forward(False, x, (ROW_D + 1,))

        collect(1, lambda dx, dy, g: g == 1)

        @pl.loop(3, 7)
        def _(x):
            z_forward(False, x, (ROW_A,))

        collect(1, lambda dx, dy, g: g == 0 and dy == 0)

        @pl.loop(0, 6)
        def _(t):
            z_forward(False, jnp.where(t < 3, t, t + 4), (ROW_A, ROW_D + 1))

        element(0, False)
        z_backward((ROW_A,))
        post(2, PA, lambda dx, dy, g: g == 0)
        collect(1, lambda dx, dy, g: g == 0 and dy != 0)

        @pl.loop(0, ORDER)
        def _(x):
            z_forward(False, x, (ROW_C,))

        element(1, True)
        z_backward((ROW_D, ROW_C))
        post(2, PA, lambda dx, dy, g: g == 1)

        @pl.loop(0, ORDER)
        def _(x):
            for k in range(LX // 8):
                row = pl.multiple_of(x * LX + 8 * k, 8)
                U[pl.ds(row + LX, 8), :] = U[pl.ds(row + LX, 8), :] + PA[pl.ds(row, 8), :]

        collect(2, lambda dx, dy, g: g == 0)
        collect(2, lambda dx, dy, g: g == 1)

        weights = [((NODES - 1 - t) / (NODES - 1), t / (NODES - 1)) for t in range(NODES)]
        coefs = [
            [jnp.broadcast_to(cc[4 * h + c : 4 * h + c + 1, :], (8, EZ)) for c in range(4)]
            for h in range(EY)
        ]

        def last(x, carry):
            wx = x.astype(F32) * (1.0 / (NODES - 1))
            carry = list(carry)
            for h in range(EY):
                r = residual(x + 1, 2 + 8 * h, coefs[h])
                for z in range(NODES):
                    ro[pl.ds(x * LX + z * WY + 8 * h, 8), :] = r[z]
                for c in range(2):
                    total = None
                    for z in range(NODES):
                        if weights[z][c] == 0.0:
                            continue
                        term = weights[z][c] * r[z]
                        total = term if total is None else total + term
                    carry[4 * h + c] = carry[4 * h + c] + (1.0 - wx) * total
                    carry[4 * h + 2 + c] = carry[4 * h + 2 + c] + wx * total
            return tuple(carry)

        acc = lax.fori_loop(0, NODES, last, tuple([zero_tile] * 8))
        wy1 = sub.astype(F32) * (1.0 / (NODES - 1))
        for h in range(EY):
            for a in range(2):
                for b in range(2):
                    for c in range(2):
                        w = wy1 if b else 1.0 - wy1
                        row = jnp.sum(acc[4 * h + 2 * a + c] * w, axis=0, keepdims=True)
                        v = 4 * a + 2 * b + c
                        mo[v : v + 1, EZ * h : EZ * (h + 1)] = row
        moments = exact_dot(mo[...], perm[...], 0)
        groups = GRP_DEV * n_sy
        column = group[...] - i * groups
        onehot = jnp.where(
            lax.broadcasted_iota(jnp.int32, (groups, EY * EZ), 0) == column, 1.0, 0.0
        ).astype(BF16)
        partial = exact_dot(moments, onehot, 1)
        per = EZ // GRP_DEV
        for d in range(n_sy):
            block = partial[:, (d // per) * EZ : (d // per + 1) * EZ]
            shift = (d % per) * GRP_DEV
            sb[d] = block if shift == 0 else pltpu.roll(block, EZ - shift, 1)

        def copy4(d):
            dest = lax.rem(j + d, n_sy)
            return pltpu.make_async_remote_copy(
                src_ref=sb.at[dest],
                dst_ref=rb.at[d - 1],
                send_sem=s4.at[d - 1],
                recv_sem=r4.at[d - 1],
                device_id=(i, dest),
                device_id_type=MESH,
            )

        for d in range(1, n_sy):
            copy4(d).start()

        def slots(ref, base):
            halves = [
                jnp.concatenate(
                    [ref[pl.ds(base + 8 * h + y, 8, stride=WY), :] for y in range(8)], axis=0
                )
                for h in range(EY)
            ]
            return exact_dot(jnp.concatenate(halves, axis=1), perm[...], 0)

        @pl.loop(0, NODES)
        def _(x):
            rows = pl.ds(pl.multiple_of(x * 64, 64), 64)
            sm_out[rows, :] = slots(U, (x + 2) * LX + 2)
            fr_out[rows, :] = slots(ro, x * LX)

        for r in range(len(ROUNDS)):
            for n, (dx, dy, g, tiles) in enumerate(ROUNDS[r]):

                @pl.when(exists(dx, dy))
                def _():
                    copy_of(r, n).wait_send()

        total = sb[j]
        for d in range(1, n_sy):
            copy4(d).wait()
            total = total + rb[d - 1]
        co_out[...] = total[:, 0:GRP_DEV]

    return kernel


def solution(mesh):
    n_sx, n_sy = mesh.shape["sx"], mesh.shape["sy"]
    def on_device(right_side, stretch, mass_term, slot_position, coarse_group):
        elements = right_side.shape[3]
        vmem = pl.BlockSpec(memory_space=pltpu.VMEM)
        V = lambda *shape: pltpu.VMEM(shape, F32)
        dma = lambda n: pltpu.SemaphoreType.DMA((n,))
        points = NODES**3
        scratch = [
            pltpu.VMEM((elements, elements), BF16),
            V(8, elements),
            V(8, EZ),
            V(ND, 8, EZ),
            V(4 * NQ, EZ),
            V(EY * NT * ORDER * 8, EZ),
            V(ORDER * LX, EZ),
            V((ORDER + 2) * LX, EZ),
            V(ORDER * LX, EZ),
            V(ORDER * NQ, EZ),
            V(ORDER * NQ, EZ),
            V(ORDER * NP, EZ),
            V(ORDER * NP, EZ),
            V(2 * NP, EZ),
            V(NODES * LX, EZ),
            V(8, elements),
            V(n_sy, 8, EZ),
            V(max(n_sy - 1, 1), 8, EZ),
        ]
        scratch += [
            V(points, elements),
            V(3, elements),
            V(1, elements),
            pltpu.VMEM((1, elements), jnp.int32),
            pltpu.VMEM((1, elements), jnp.int32),
            V(3 * NP + 4, EZ),
            dma(5),
        ]
        for messages in ROUNDS:
            for side in range(2):
                scratch += [V(8 * message_size(m), EZ) for m in messages]
            scratch += [dma(len(messages))] * 2
        scratch += [dma(max(n_sy - 1, 1))] * 2
        smoothed, fine, coarse = pl.pallas_call(
            make_kernel(n_sx, n_sy),
            out_shape=(
                jax.ShapeDtypeStruct((points, elements), F32),
                jax.ShapeDtypeStruct((points, elements), F32),
                jax.ShapeDtypeStruct((8, GRP_DEV), F32),
            ),
            in_specs=[pl.BlockSpec(memory_space=pltpu.HBM)] * 5,
            out_specs=(vmem, vmem, vmem),
            scratch_shapes=scratch,
            compiler_params=pltpu.CompilerParams(
                collective_id=0, has_side_effects=True, vmem_limit_bytes=48 * 1024 * 1024
            ),
        )(
            *(
                pltpu.with_memory_space_constraint(array, pltpu.HBM)
                for array in (
                    right_side.reshape(points, elements),
                    stretch,
                    mass_term.reshape(1, elements),
                    slot_position.reshape(1, elements),
                    coarse_group.reshape(1, elements),
                )
            ),
        )
        shape = right_side.shape
        return smoothed.reshape(shape), fine.reshape(shape), coarse

    split = ("sx", "sy")
    field = P(None, None, None, split)
    return jax.shard_map(
        on_device,
        mesh=mesh,
        in_specs=(field, P(None, split), P(split), P(split), P(split)),
        out_specs=(field, field, P(None, split)),
        check_vma=False,
    )
```
